768 devices in a mesh: seq: 48 (over z, x), chan: 16 (over y, core).
Axes of the slice: x: 4, y: 8, z: 12, core: 2. Of those that a mesh axis runs over, the one named last changes fastest.
Arguments:
- query_in: bfloat16 [6144, 2048], P('seq', 'chan'), may hold values from -6 to 6
- key_in: bfloat16 [6144, 2048], P('seq', 'chan'), may hold values from -6 to 6
- value_in: bfloat16 [6144, 2048], P('seq', 'chan'), may hold values from -6 to 6
- short_taps: float32 [3, 7, 2048], P(None, None, 'chan'), may hold values from -2 to 2
- long_filters: bfloat16 [128, 6144], P('chan'), may hold values from -1.1 to 1.1
- skip_gain: float32 [2048], P('chan'), may hold values from -1 to 1
- cotangent: bfloat16 [6144, 2048], P('seq', 'chan'), may hold values from -6 to 6
Outputs:
- block_out: bfloat16 [6144, 2048], P('seq', 'chan')
- input_grads: bfloat16 [3, 6144, 2048], P(None, 'seq', 'chan')
- tap_grads: float32 [3, 7, 2048], P(None, None, 'chan')
- skip_grad: float32 [2048], P('chan')
- filter_grad: float32 [128, 6144], P('chan')
The draws below stay inside these ranges and needn't reach their ends.
All inputs are finite; a program needn't handle non-finite values.
Results may differ from the reference program's by a relative error of at most 0.0085.
Values may be sent and summed in bfloat16 or wider, within the bound.
A program may use at most 128 MiB of HBM per device.

```python
import math
import jax
import jax.numpy as jnp
from jax import lax

GROUP = 16
TAPS = 7
CH = 2048
GROUPS = 128
SEQ_LEN = 6144


def draw_long_filters(key, part):
    subkeys = jax.random.split(key, 4)
    lag_axis = jnp.arange(SEQ_LEN, dtype=jnp.float32)
    slow_rate = jax.random.uniform(subkeys[0], (GROUPS, 1), jnp.float32, 0.3, 2.0) / SEQ_LEN
    fast_rate = 1.0 / jax.random.uniform(subkeys[1], (GROUPS, 1), jnp.float32, 30.0, 50.0)
    fast_share = 0.5
    rough_part = jax.random.truncated_normal(subkeys[3], -4.0, 4.0, (GROUPS, SEQ_LEN), jnp.float32)
    chosen = jax.random.uniform(subkeys[2], (GROUPS, 1), jnp.float32) < fast_share
    decay_rate = jnp.where(chosen, fast_rate, slow_rate)
    energy = jnp.sqrt(jnp.expm1(-2.0 * decay_rate * SEQ_LEN) / jnp.expm1(-2.0 * decay_rate))
    return (jnp.exp(-decay_rate * lag_axis) * rough_part / energy).astype(jnp.bfloat16)


def block_levels(rng, shape, pieces, low, high):
    factor_of, own = 1.0, jax.random.fold_in(rng, 6)
    for dim, parts in pieces:
        steps = jnp.exp(jax.random.uniform(jax.random.fold_in(own, dim), (parts,), jnp.float32, low / len(pieces), high / len(pieces)))
        factor_of = factor_of * jnp.repeat(steps, shape[dim] // parts).reshape([-1 if axis == dim else 1 for axis in range(len(shape))])
    return factor_of


def scatter_about(stream_key, shape, deviation, reach, shards=(), kind=jnp.bfloat16):
    entries = jax.random.normal(stream_key, shape, jnp.float32) * deviation
    if len(shards) > 0:
        entries = block_levels(stream_key, shape, shards, -0.22, 0.18) * entries
    return jnp.clip(entries, min=-reach, max=reach).astype(kind)


def setup_inputs(seed: int = 0) -> dict:
    arg_keys = jax.random.split(jax.random.key(seed), 8)
    return {
        "query_in": scatter_about(arg_keys[0], (SEQ_LEN, CH), 1.0, 6.0, ((0, 48), (1, 16))),
        "key_in": scatter_about(arg_keys[1], (SEQ_LEN, CH), 1.0, 6.0, ((0, 48), (1, 16))),
        "value_in": scatter_about(arg_keys[2], (SEQ_LEN, CH), 1.0, 6.0, ((0, 48), (1, 16))),
        "short_taps": scatter_about(arg_keys[3], (3, TAPS, CH), TAPS ** -0.5, 2.0, ((2, 16),), jnp.float32),
        "long_filters": draw_long_filters(jax.random.fold_in(arg_keys[7], 71), 0),
        "skip_gain": jnp.clip(jax.random.uniform(arg_keys[5], (CH,), jnp.float32, -1.0, 1.0) * block_levels(arg_keys[5], (CH,), ((0, 16),), -0.4, 0.0), -1.0, 1.0),
        "cotangent": scatter_about(arg_keys[6], (SEQ_LEN, CH), 1.0, 6.0, ((0, 48), (1, 16))),
    }


def delayed(signal, offset):
    return jnp.pad(signal, ((offset, 0), (0, 0)))[:signal.shape[0]]

def advanced(signal, offset):
    return jnp.pad(signal, ((0, offset), (0, 0)))[offset:]

def reference(query_in, key_in, value_in, short_taps, long_filters, skip_gain, cotangent):
    inputs = [query_in.astype(jnp.float32), key_in.astype(jnp.float32), value_in.astype(jnp.float32)]
    shorts = []
    for stream in range(3):
        running = jnp.zeros_like(inputs[stream])
        for offset in range(TAPS):
            running = running + short_taps[stream, offset] * delayed(inputs[stream], offset)
        shorts.append(running)
    query_short, key_short, value_short = shorts
    gating = (key_short * value_short).astype(jnp.bfloat16)
    relayed = (cotangent.astype(jnp.float32) * query_short).astype(jnp.bfloat16)
    gating_wide = gating.astype(jnp.float32)
    relayed_wide = relayed.astype(jnp.float32)
    length = 2 * SEQ_LEN
    gating_groups = gating_wide.T.reshape(GROUPS, GROUP, SEQ_LEN)
    relayed_groups = relayed_wide.T.reshape(GROUPS, GROUP, SEQ_LEN)

    def per_group(members):
        gating_row, relayed_row, filter_row = members
        filter_spec = jnp.fft.rfft(filter_row, length)
        gating_spec = jnp.fft.rfft(gating_row, length, axis=-1)
        relayed_spec = jnp.fft.rfft(relayed_row, length, axis=-1)
        forward = jnp.fft.irfft(gating_spec * filter_spec[None, :], length, axis=-1)[:, :SEQ_LEN]
        backward = jnp.fft.irfft(relayed_spec * jnp.conj(filter_spec)[None, :], length, axis=-1)[:, :SEQ_LEN]
        lag_sums = jnp.fft.irfft(lax.optimization_barrier(jnp.sum(relayed_spec * jnp.conj(gating_spec), axis=0)), length)[:SEQ_LEN]
        return (forward, backward, lag_sums)
    forward, backward, lag_sums = lax.map(per_group, (gating_groups, relayed_groups, long_filters.astype(jnp.float32)))
    long_out = forward.reshape(CH, SEQ_LEN).T + skip_gain * gating_wide
    block_out = (query_short * long_out).astype(jnp.bfloat16)
    cot_wide = cotangent.astype(jnp.float32)
    grad_gating = backward.reshape(CH, SEQ_LEN).T + skip_gain * relayed_wide
    grad_shorts = [cot_wide * long_out, grad_gating * value_short, grad_gating * key_short]
    input_list = []
    tap_list = []
    for stream in range(3):
        running = jnp.zeros_like(grad_shorts[stream])
        tap_terms = []
        for offset in range(TAPS):
            running = running + short_taps[stream, offset] * advanced(grad_shorts[stream], offset)
            tap_terms.append(lax.optimization_barrier(jnp.sum(grad_shorts[stream] * delayed(inputs[stream], offset), axis=0)))
        input_list.append(running)
        tap_list.append(jnp.stack(tap_terms))
    input_grads = jnp.stack(input_list).astype(jnp.bfloat16)
    tap_scale = 1.0 / math.sqrt(SEQ_LEN)
    tap_grads = jnp.stack(tap_list) * tap_scale
    skip_grad = lax.optimization_barrier(jnp.sum(relayed_wide * gating_wide, axis=0)) * tap_scale
    filter_grad = lag_sums * (1.0 / math.sqrt(SEQ_LEN * GROUP))
    return (block_out, input_grads, tap_grads, skip_grad, filter_grad)
```

```python
import math

import jax
import jax.numpy as jnp
from jax import lax
from jax.experimental import pallas as pl
from jax.experimental.pallas import tpu as pltpu
from jax.sharding import PartitionSpec as P

F32 = jnp.float32
BF16 = jnp.bfloat16
MESH = pl.DeviceIdType.MESH

BLK = 128
NB = 48
NW = 32
TAPS = 7
NG = 8
QUART = NB // 4
PAIRS = NB // 2


def worker_of(index):
    z, x = index // 4, index % 4
    return ((z // 3) * 2 + z % 3) * 4 + x


def is_worker(index):
    return (index // 4) % 3 != 2


def index_of(worker):
    group, x = worker // 4, worker % 4
    return ((group // 2) * 3 + group % 2) * 4 + x


def iota(shape, dim):
    return lax.broadcasted_iota(jnp.int32, shape, dim)


def dot(a, b, dims=((1,), (0,))):
    return lax.dot_general(a, b, (dims, ((), ())), preferred_element_type=F32)


def half_turn(x):
    return pltpu.roll(x, 4, 0)


def remote(src, dst, send_sem, recv_sem, target):
    return pltpu.make_async_remote_copy(
        src_ref=src,
        dst_ref=dst,
        send_sem=send_sem,
        recv_sem=recv_sem,
        device_id={"seq": target},
        device_id_type=MESH,
    )


def kernel(
    q_ref, k_ref, v_ref, c_ref, taps_ref, filt_ref, skip_ref,
    out_ref, ig_ref, tapg_ref, skipg_ref, fg_ref,
    perm, sendb, recvb, toep, tcol, conv_s, pb_s, pbj_s, r8_s, gg_s, z_s, y_s, yj_s,
    retb, retr, small, smallr, sm_s, fbuf, frecv, fq, fgbuf,
    in_send, in_recv, ret_send, ret_recv, sm_send, sm_recv,
    fr_send, fr_recv, fb_send, fb_recv,
):
    me = lax.axis_index("seq")
    mine = worker_of(me)
    group = mine // 4
    part = me % 4
    tap_scale = 1.0 / math.sqrt(NB * BLK)
    lag_scale = 1.0 / math.sqrt(NB * BLK * 16)

    barrier = pltpu.get_barrier_semaphore()

    def greet(i, carry):
        pl.semaphore_signal(
            barrier, inc=1, device_id={"seq": lax.rem(me + i, NB)}, device_id_type=MESH
        )
        return carry

    lax.fori_loop(1, NB, greet, 0)

    rho = iota((512, 1), 0)
    target_col = 128 * ((rho // 4) % 4) + 4 * (rho // 16) + rho % 4
    perm[...] = jnp.where(iota((512, 512), 1) == target_col, 1.0, 0.0).astype(BF16)
    streams = jnp.concatenate([q_ref[...], k_ref[...], c_ref[...], v_ref[...]], axis=1)
    sendb[...] = dot(perm[...], streams, ((1,), (1,))).astype(BF16).reshape(NW, 16, BLK)

    pl.semaphore_wait(barrier, NB - 1)

    def send_in(i, carry):
        target = lax.rem(me + i, NB)

        @pl.when(is_worker(target))
        def _():
            worker = worker_of(target)
            remote(
                sendb.at[worker], recvb.at[me], in_send.at[worker], in_recv.at[me], target
            ).start()

        return carry

    lax.fori_loop(1, NB, send_in, 0)

    @pl.when(is_worker(me))
    def _work():
        lane = iota((16, BLK), 1)
        row = iota((16, BLK), 0)
        low_rows = iota((8, BLK), 0) < 4

        own = lane == 4 * mine + row % 4
        for j in range(TAPS):
            q_tap = jnp.broadcast_to(taps_ref[0, j : j + 1, :], (16, BLK))
            k_tap = jnp.broadcast_to(taps_ref[1, j : j + 1, :], (16, BLK))
            v_tap = jnp.broadcast_to(taps_ref[2, j : j + 1, :], (16, BLK))
            tap = jnp.where(row < 4, q_tap, jnp.where(row < 8, k_tap, v_tap))
            column = jnp.sum(jnp.where(own, tap, 0.0), axis=1, keepdims=True)
            column = jnp.broadcast_to(column, (16, BLK))
            unit = 1.0 if j == 0 else 0.0
            tcol[j] = jnp.where((row >= 8) & (row < 12), unit, column)
        skip_own = jnp.where(own, jnp.broadcast_to(skip_ref[...], (16, BLK)), 0.0)
        skip_col = jnp.broadcast_to(jnp.sum(skip_own, axis=1, keepdims=True), (16, BLK))[:8]

        square_row = iota((BLK, BLK), 0)
        square_lane = iota((BLK, BLK), 1)
        toep[0] = jnp.zeros((BLK, BLK), BF16)

        def build(n, previous):
            rows = filt_ref[:, pl.ds(pl.multiple_of(n * BLK, BLK), BLK)].astype(F32)
            line = jnp.sum(jnp.where(iota((NG, BLK), 0) == group, rows, 0.0), axis=0, keepdims=True)
            turned = pltpu.roll(
                jnp.broadcast_to(line, (BLK, BLK)), 0, 1, stride=1, stride_axis=0
            )
            toep[n + 1] = jnp.where(square_lane >= square_row, turned, previous).astype(BF16)
            return turned

        lax.fori_loop(0, NB, build, jnp.zeros((BLK, BLK), F32))
        flip = jnp.where(square_row + square_lane == BLK - 1, 1.0, 0.0).astype(BF16)

        r8_s[PAIRS:] = jnp.zeros((32 - PAIRS, 8, BLK), F32)
        gg_s[:PAIRS] = jnp.zeros((PAIRS, 8, 2 * BLK), F32)
        gg_s[2 * PAIRS :] = jnp.zeros((32 - PAIRS, 8, 2 * BLK), F32)
        y_s[...] = jnp.zeros((2 * PAIRS, 8, 2 * BLK), F32)
        pbj_s[0] = jnp.zeros((8, BLK), F32)

        recvb[me] = sendb[mine]

        def short(b, before):
            @pl.when(b != me)
            def _():
                remote(
                    sendb.at[0], recvb.at[b], in_send.at[0], in_recv.at[b], b
                ).wait_recv()

            x = recvb[b].astype(F32)
            total = tcol[0] * x
            turned = []
            for j in range(1, TAPS):
                t = pltpu.roll(x, j, 1)
                total = total + tcol[j] * jnp.where(lane < j, before[j - 1], t)
                turned.append(t)
            conv_s[b] = total
            pb_s[b] = (total[:8] * total[8:]).astype(BF16).astype(F32)
            return tuple(turned)

        empty = tuple(jnp.zeros((16, BLK), F32) for _ in range(TAPS - 1))
        lax.fori_loop(0, NB, short, empty)

        pbj_s[1:] = dot(pb_s[...].reshape(NB * 8, BLK).astype(BF16), flip).reshape(NB, 8, BLK)

        def arrange(e, carry):
            p0, p1 = pb_s[2 * e], pb_s[2 * e + 1]
            jm, j0, j1 = pbj_s[2 * e], pbj_s[2 * e + 1], pbj_s[2 * e + 2]
            r8_s[e] = jnp.where(low_rows, p0, half_turn(p1))
            gg_s[PAIRS + e, :, :BLK] = jnp.where(low_rows, half_turn(j0), j1)
            gg_s[PAIRS + e, :, BLK:] = jnp.where(low_rows, half_turn(jm), j0)
            z_s[e, :, :BLK] = jnp.where(low_rows, pbj_s[NB - 2 * e], p0)
            z_s[e, :, BLK:] = jnp.where(low_rows, pbj_s[NB - 1 - 2 * e], p1)
            return carry

        lax.fori_loop(0, PAIRS, arrange, 0)

        unit = jnp.where(square_row == square_lane, 1.0, 0.0).astype(BF16)
        r8_t = dot(unit, r8_s[...].reshape(256, BLK).astype(BF16), ((1,), (1,))).astype(BF16)
        inside = square_lane <= square_row

        def lags(f, previous):
            shifted = gg_s[pl.ds(PAIRS - f, 32)].reshape(256, 2 * BLK).astype(BF16)
            product = dot(r8_t, shifted)
            even = pltpu.roll(product[:, :BLK], 1, 1, stride=1, stride_axis=0)
            odd = pltpu.roll(product[:, BLK:], 1, 1, stride=1, stride_axis=0)
            fbuf[2 * f] = jnp.sum(jnp.where(inside, previous, even), axis=0, keepdims=True)
            fbuf[2 * f + 1] = jnp.sum(jnp.where(inside, even, odd), axis=0, keepdims=True)
            return odd

        last = lax.fori_loop(0, PAIRS, lags, jnp.zeros((BLK, BLK), F32))
        fbuf[NB] = jnp.sum(jnp.where(inside, last, 0.0), axis=0, keepdims=True)

        def send_lags(i, carry):
            other = lax.rem(part + i, 4)
            remote(
                fbuf.at[pl.ds(1 + QUART * other, QUART)], frecv.at[part],
                fr_send.at[other], fr_recv.at[part], me - part + other,
            ).start()
            return carry

        lax.fori_loop(1, 4, send_lags, 0)

        z = z_s[...].reshape(PAIRS * 8, 2 * BLK).astype(BF16)

        def convolve(d, carry):
            t0, t1, t2 = toep[2 * d], toep[2 * d + 1], toep[2 * d + 2]
            weights = jnp.concatenate(
                [jnp.concatenate([t1, t2], axis=1), jnp.concatenate([t0, t1], axis=1)], axis=0
            )
            y_s[pl.ds(d, PAIRS)] += dot(z, weights).reshape(PAIRS, 8, 2 * BLK)
            return carry

        lax.fori_loop(0, PAIRS, convolve, 0)

        for half in range(2):
            y = y_s[:PAIRS, :, half * BLK : (half + 1) * BLK].reshape(PAIRS * 8, BLK)
            high = y.astype(BF16)
            rest = (y - high.astype(F32)).astype(BF16)
            yj_s[:, :, half * BLK : (half + 1) * BLK] = (
                dot(high, flip) + dot(rest, flip)
            ).reshape(PAIRS, 8, BLK)

        def finish(b, y, yj, after, sums, skip_sum):
            p = pb_s[b]
            u = half_turn(jnp.where(low_rows, yj, y) + skip_col * p)
            short_tile = conv_s[b]
            he = jnp.concatenate([short_tile[8:] * u, short_tile[:8] * u], axis=0)
            x = recvb[b].astype(F32)
            total = tcol[0] * he
            new_sums = [sums[0] + he * x]
            turned = []
            for j in range(1, TAPS):
                t = pltpu.roll(he, BLK - j, 1)
                s = jnp.where(lane < BLK - j, t, after[j - 1])
                total = total + tcol[j] * s
                new_sums.append(sums[j] + s * x)
                turned.append(t)
            retb[b] = total.astype(BF16)
            return tuple(turned), tuple(new_sums), skip_sum + p * half_turn(p)

        def send_back(b):
            @pl.when(b != me)
            def _():
                remote(retb.at[b], retr.at[mine], ret_send.at[b], ret_recv.at[mine], b).start()

        def post(i, carry):
            after, sums, skip_sum = carry
            e = PAIRS - 1 - i
            after, sums, skip_sum = finish(
                2 * e + 1, y_s[e, :, BLK:], yj_s[i, :, :BLK], after, sums, skip_sum
            )
            after, sums, skip_sum = finish(
                2 * e, y_s[e, :, :BLK], yj_s[i, :, BLK:], after, sums, skip_sum
            )
            return after, sums, skip_sum

        start = (
            empty,
            tuple(jnp.zeros((16, BLK), F32) for _ in range(TAPS)),
            jnp.zeros((8, BLK), F32),
        )
        _, sums, skip_sum = lax.fori_loop(0, PAIRS, post, start)

        def return_block(i, carry):
            send_back(lax.rem(me + i, NB))
            return carry

        lax.fori_loop(1, NB, return_block, 0)

        line = jnp.zeros((16, BLK), F32)
        for j in range(TAPS):
            line = line + jnp.where(
                lane == 16 * j + row, jnp.sum(sums[j], axis=1, keepdims=True), 0.0
            )
        skip_line = jnp.where(
            lane[:8] == 16 * TAPS + row[:8], jnp.sum(skip_sum, axis=1, keepdims=True), 0.0
        )
        small[...] = tap_scale * (
            jnp.sum(line, axis=0, keepdims=True) + jnp.sum(skip_line, axis=0, keepdims=True)
        )

        frecv[part] = fbuf[pl.ds(1 + QUART * part, QUART)]

        def wait_lags(i, carry):
            other = lax.rem(part + i, 4)
            remote(
                fbuf.at[pl.ds(0, QUART)], frecv.at[other],
                fr_send.at[0], fr_recv.at[other], me - part + other,
            ).wait_recv()
            return carry

        lax.fori_loop(1, 4, wait_lags, 0)
        fq[...] = lag_scale * ((frecv[0] + frecv[1]) + (frecv[2] + frecv[3]))

        def broadcast(i, carry):
            target = lax.rem(me + i, NB)
            remote(small, smallr.at[mine], sm_send.at[target], sm_recv.at[mine], target).start()
            remote(
                fq, fgbuf.at[group, pl.ds(QUART * part, QUART)],
                fb_send.at[target], fb_recv.at[mine], target,
            ).start()
            return carry

        lax.fori_loop(1, NB, broadcast, 0)
        retr[mine] = retb[me]
        smallr[mine] = small[...]
        fgbuf[group, pl.ds(QUART * part, QUART)] = fq[...]

    def wait_back(m, carry):
        source = index_of(m)

        @pl.when(source != me)
        def _():
            remote(retb.at[0], retr.at[m], ret_send.at[0], ret_recv.at[m], source).wait_recv()

        return carry

    lax.fori_loop(0, NW, wait_back, 0)
    back = dot(retr[...].reshape(512, BLK), perm[...], ((0,), (0,))).astype(BF16)
    ig_ref[0] = back[:, 0:128]
    ig_ref[1] = back[:, 128:256]
    out_ref[...] = back[:, 256:384]
    ig_ref[2] = back[:, 384:512]

    def wait_small(m, carry):
        source = index_of(m)

        @pl.when(source != me)
        def _():
            remote(small, smallr.at[m], sm_send.at[0], sm_recv.at[m], source).wait_recv()
            remote(
                fq, fgbuf.at[m // 4, pl.ds(QUART * (m % 4), QUART)],
                fb_send.at[0], fb_recv.at[m], source,
            ).wait_recv()

        return carry

    lax.fori_loop(0, NW, wait_small, 0)

    sm_s[...] = jnp.zeros((BLK, BLK), F32)
    for m in range(NW):
        sm_s[m : m + 1, :] = smallr[m]
    select = jnp.where(iota((BLK, BLK), 0) == iota((BLK, BLK), 1) // 4, 1.0, 0.0)
    spread = lax.dot_general(
        sm_s[...].T, select, (((1,), (0,)), ((), ())),
        precision=lax.Precision.HIGHEST, preferred_element_type=F32,
    ).reshape(8, 16, BLK)
    row3 = iota((8, 16, BLK), 1)
    channel = iota((8, 16, BLK), 2) % 4
    for stream, first in enumerate((0, 4, 12)):
        picked = jnp.sum(jnp.where(row3 == channel + first, spread, 0.0), axis=1)
        tapg_ref[stream] = picked[:TAPS]
        if stream == 0:
            skipg_ref[...] = picked[TAPS:]

    def lay(n, carry):
        for g in range(NG):
            fg_ref[g : g + 1, pl.ds(pl.multiple_of(n * BLK, BLK), BLK)] = fgbuf[g, n]
        return carry

    lax.fori_loop(0, NB, lay, 0)

    def drain_in(i, carry):
        target = lax.rem(me + i, NB)

        @pl.when(is_worker(target))
        def _():
            worker = worker_of(target)
            remote(
                sendb.at[worker], recvb.at[me], in_send.at[worker], in_recv.at[me], target
            ).wait_send()

        return carry

    lax.fori_loop(1, NB, drain_in, 0)

    @pl.when(is_worker(me))
    def _drain():
        def drain_lags(i, carry):
            other = lax.rem(part + i, 4)
            remote(
                fbuf.at[pl.ds(1 + QUART * other, QUART)], frecv.at[part],
                fr_send.at[other], fr_recv.at[part], me - part + other,
            ).wait_send()
            return carry

        lax.fori_loop(1, 4, drain_lags, 0)

        def drain(i, carry):
            target = lax.rem(me + i, NB)
            remote(
                retb.at[target], retr.at[mine], ret_send.at[target], ret_recv.at[mine], target
            ).wait_send()
            remote(
                small, smallr.at[mine], sm_send.at[target], sm_recv.at[mine], target
            ).wait_send()
            remote(
                fq, fgbuf.at[group, pl.ds(QUART * part, QUART)],
                fb_send.at[target], fb_recv.at[mine], target,
            ).wait_send()
            return carry

        lax.fori_loop(1, NB, drain, 0)


def local(query_in, key_in, value_in, short_taps, long_filters, skip_gain, cotangent):
    vmem = pl.BlockSpec(memory_space=pltpu.VMEM)
    dma = pltpu.SemaphoreType.DMA
    results = pl.pallas_call(
        kernel,
        out_shape=(
            jax.ShapeDtypeStruct((BLK, BLK), BF16),
            jax.ShapeDtypeStruct((3, BLK, BLK), BF16),
            jax.ShapeDtypeStruct((3, TAPS, BLK), F32),
            jax.ShapeDtypeStruct((1, BLK), F32),
            jax.ShapeDtypeStruct((NG, NB * BLK), F32),
        ),
        in_specs=[vmem] * 7,
        out_specs=(vmem,) * 5,
        scratch_shapes=[
            pltpu.VMEM((512, 512), BF16),
            pltpu.VMEM((NW, 16, BLK), BF16),
            pltpu.VMEM((NB, 16, BLK), BF16),
            pltpu.VMEM((NB + 1, BLK, BLK), BF16),
            pltpu.VMEM((TAPS, 16, BLK), F32),
            pltpu.VMEM((NB, 16, BLK), F32),
            pltpu.VMEM((NB, 8, BLK), F32),
            pltpu.VMEM((NB + 1, 8, BLK), F32),
            pltpu.VMEM((32, 8, BLK), F32),
            pltpu.VMEM((PAIRS + 32, 8, 2 * BLK), F32),
            pltpu.VMEM((PAIRS, 8, 2 * BLK), F32),
            pltpu.VMEM((2 * PAIRS, 8, 2 * BLK), F32),
            pltpu.VMEM((PAIRS, 8, 2 * BLK), F32),
            pltpu.VMEM((NB, 16, BLK), BF16),
            pltpu.VMEM((NW, 16, BLK), BF16),
            pltpu.VMEM((1, BLK), F32),
            pltpu.VMEM((NW, 1, BLK), F32),
            pltpu.VMEM((BLK, BLK), F32),
            pltpu.VMEM((NB + 1, 1, BLK), F32),
            pltpu.VMEM((4, QUART, 1, BLK), F32),
            pltpu.VMEM((QUART, 1, BLK), F32),
            pltpu.VMEM((NG, NB, 1, BLK), F32),
            dma((NW,)), dma((NB,)), dma((NB,)), dma((NW,)), dma((NB,)), dma((NW,)),
            dma((4,)), dma((4,)), dma((NB,)), dma((NW,)),
        ],
        compiler_params=pltpu.CompilerParams(collective_id=0, has_side_effects=True),
        name="hyena",
    )(query_in, key_in, value_in, cotangent, short_taps, long_filters, skip_gain.reshape(1, BLK))
    block_out, input_grads, tap_grads, skip_grad, filter_grad = results
    return block_out, input_grads, tap_grads, skip_grad.reshape(BLK), filter_grad


def solution(mesh):
    in_specs = (
        P("seq", "chan"),
        P("seq", "chan"),
        P("seq", "chan"),
        P(None, None, "chan"),
        P("chan", None),
        P("chan"),
        P("seq", "chan"),
    )
    out_specs = (
        P("seq", "chan"),
        P(None, "seq", "chan"),
        P(None, None, "chan"),
        P("chan"),
        P("chan", None),
    )
    return jax.shard_map(local, mesh=mesh, in_specs=in_specs, out_specs=out_specs, check_vma=False)
```

```python
import math

import jax
import jax.numpy as jnp
from jax import lax
from jax.experimental import pallas as pl
from jax.experimental.pallas import tpu as pltpu
from jax.sharding import PartitionSpec as P

F32 = jnp.float32
BF16 = jnp.bfloat16
MESH = pl.DeviceIdType.MESH

BLK = 128
NB = 48
NW = 32
TAPS = 7
NG = 8
QUART = NB // 4
PAIRS = NB // 2


def iota(shape, dim):
    return lax.broadcasted_iota(jnp.int32, shape, dim)


def dot(a, b, dims=((1,), (0,))):
    return lax.dot_general(a, b, (dims, ((), ())), preferred_element_type=F32)


def half_turn(x):
    return pltpu.roll(x, 4, 0)


def remote(src, dst, send_sem, recv_sem, target):
    return pltpu.make_async_remote_copy(
        src_ref=src,
        dst_ref=dst,
        send_sem=send_sem,
        recv_sem=recv_sem,
        device_id={"seq": target},
        device_id_type=MESH,
    )


def wait_for(ref, sem):
    pltpu.make_async_copy(ref, ref, sem).wait()


def transposer():
    rho = iota((512, 1), 0)
    column = 128 * ((rho // 4) % 4) + 4 * (rho // 16) + rho % 4
    return jnp.where(iota((512, 512), 1) == column, 1.0, 0.0).astype(BF16)


def kernel(
    q_hbm, k_hbm, c_hbm, v_hbm, taps_hbm, filt_hbm, skip_hbm,
    back_hbm, small_hbm, fg_hbm,
    streams, taps_ref, filt_ref, skip_ref,
    perm, sendb, recvb, toep, tcol, conv_s, pb_s, r8_s, gg_s, z_s, y_s, yj_s,
    retb, retr, small, smallr, fbuf, frecv, fq, fgbuf,
    load_sem, out_sem, in_send, in_recv, ret_send, ret_recv, sm_send, sm_recv,
    fr_send, fr_recv, fb_send, fb_recv,
):
    me = lax.axis_index("seq")
    plane = me // 4
    part = me % 4
    tap_scale = 1.0 / math.sqrt(NB * BLK)
    lag_scale = 1.0 / math.sqrt(NB * BLK * 16)
    working = me < NW
    barrier = pltpu.get_barrier_semaphore()

    loads = [
        pltpu.make_async_copy(source, streams.at[r], load_sem.at[r])
        for r, source in enumerate((q_hbm, k_hbm, c_hbm, v_hbm))
    ]
    for load in loads:
        load.start()
    own_loads = [
        pltpu.make_async_copy(taps_hbm, taps_ref, load_sem.at[4]),
        pltpu.make_async_copy(filt_hbm, filt_ref, load_sem.at[5]),
        pltpu.make_async_copy(skip_hbm, skip_ref, load_sem.at[6]),
    ]

    @pl.when(working)
    def _greet():
        for load in own_loads:
            load.start()

        def greet(i, carry):
            pl.semaphore_signal(
                barrier, inc=1, device_id={"seq": lax.rem(me + i, NB)}, device_id_type=MESH
            )
            return carry

        lax.fori_loop(1, NB, greet, 0)

    perm[...] = transposer()
    for load in loads:
        load.wait()
    joined = jnp.concatenate([streams[r] for r in range(4)], axis=1)
    sendb[...] = dot(perm[...], joined, ((1,), (1,))).astype(BF16).reshape(NW, 16, BLK)

    lane = iota((16, BLK), 1)
    row = iota((16, BLK), 0)
    low_rows = iota((8, BLK), 0) < 4
    square_row = iota((BLK, BLK), 0)
    square_lane = iota((BLK, BLK), 1)
    identity = jnp.where(square_row == square_lane, 1.0, 0.0).astype(BF16)
    flip = jnp.where(square_row + square_lane == BLK - 1, 1.0, 0.0).astype(BF16)

    @pl.when(working)
    def _prepare():
        for load in own_loads:
            load.wait()

        own = lane == 4 * me + row % 4
        for j in range(TAPS):
            q_tap = jnp.broadcast_to(taps_ref[0, j : j + 1, :], (16, BLK))
            k_tap = jnp.broadcast_to(taps_ref[1, j : j + 1, :], (16, BLK))
            v_tap = jnp.broadcast_to(taps_ref[2, j : j + 1, :], (16, BLK))
            tap = jnp.where(row < 4, q_tap, jnp.where(row < 8, k_tap, v_tap))
            column = jnp.sum(jnp.where(own, tap, 0.0), axis=1, keepdims=True)
            column = jnp.broadcast_to(column, (16, BLK))
            unit = 1.0 if j == 0 else 0.0
            tcol[j] = jnp.where((row >= 8) & (row < 12), unit, column)
        skip_own = jnp.where(own, jnp.broadcast_to(skip_ref[...], (16, BLK)), 0.0)
        tcol[TAPS] = jnp.broadcast_to(jnp.sum(skip_own, axis=1, keepdims=True), (16, BLK))

        toep[0] = jnp.zeros((BLK, BLK), BF16)

        def build(n, previous):
            rows = filt_ref[:, pl.ds(pl.multiple_of(n * BLK, BLK), BLK)].astype(F32)
            line = jnp.sum(jnp.where(iota((NG, BLK), 0) == plane, rows, 0.0), axis=0, keepdims=True)
            turned = pltpu.roll(
                jnp.broadcast_to(line, (BLK, BLK)), 0, 1, stride=1, stride_axis=0
            )
            toep[n + 1] = jnp.where(square_lane >= square_row, turned, previous).astype(BF16)
            return turned

        lax.fori_loop(0, NB, build, jnp.zeros((BLK, BLK), F32), unroll=2)

        r8_s[PAIRS:] = jnp.zeros((32 - PAIRS, 8, BLK), F32)
        gg_s[:PAIRS] = jnp.zeros((PAIRS, 8, 2 * BLK), F32)
        gg_s[2 * PAIRS :] = jnp.zeros((32 - PAIRS, 8, 2 * BLK), F32)
        y_s[...] = jnp.zeros((2 * PAIRS, 8, 2 * BLK), F32)
        recvb[me] = sendb[me]
        pl.semaphore_wait(barrier, NW - 1)

    @pl.when(me >= NW)
    def _():
        pl.semaphore_wait(barrier, NW)

    for m in range(NW):
        @pl.when(m != me)
        def _(m=m):
            remote(sendb.at[m], recvb.at[me], in_send, in_recv.at[plane], m).start()

    @pl.when(working)
    def _work():
        skip_col = tcol[TAPS][:8]

        def short(z, carry):
            before, jm = carry

            @pl.when(z == plane)
            def _():
                wait_for(recvb.at[pl.ds(0, 3)], in_recv.at[z])

            @pl.when(z != plane)
            def _():
                wait_for(recvb.at[pl.ds(0, 4)], in_recv.at[z])

            for b4 in range(4):
                b = 4 * z + b4
                x = recvb[b].astype(F32)
                total = tcol[0] * x
                turned = []
                for j in range(1, TAPS):
                    t = pltpu.roll(x, j, 1)
                    total = total + tcol[j] * jnp.where(lane < j, before[j - 1], t)
                    turned.append(t)
                conv_s[b] = total
                pb_s[b] = (total[:8] * total[8:]).astype(BF16).astype(F32)
                before = tuple(turned)

            pb4 = pb_s[pl.ds(4 * z, 4)]
            pj4 = dot(pb4.reshape(32, BLK).astype(BF16), flip).reshape(4, 8, BLK)
            for half in range(2):
                e = 2 * z + half
                p0, p1 = pb4[2 * half], pb4[2 * half + 1]
                j0, j1 = pj4[2 * half], pj4[2 * half + 1]
                r8_s[e] = jnp.where(low_rows, p0, half_turn(p1))
                gg_s[PAIRS + e, :, :BLK] = jnp.where(low_rows, half_turn(j0), j1)
                gg_s[PAIRS + e, :, BLK:] = jnp.where(low_rows, half_turn(jm), j0)
                z_s[e, 4:, :BLK] = p0[4:]
                z_s[e, 4:, BLK:] = p1[4:]
                z_s[PAIRS - 1 - e, :4, :BLK] = j1[:4]
                z_s[PAIRS - 1 - e, :4, BLK:] = j0[:4]
                jm = j1
            return before, jm

        empty = tuple(jnp.zeros((16, BLK), F32) for _ in range(TAPS - 1))
        lax.fori_loop(0, NB // 4, short, (empty, jnp.zeros((8, BLK), F32)))

        r8_t = dot(identity, r8_s[...].reshape(256, BLK).astype(BF16), ((1,), (1,))).astype(BF16)
        inside = square_lane <= square_row

        def lags(f, previous):
            shifted = gg_s[pl.ds(PAIRS - f, 32)].reshape(256, 2 * BLK).astype(BF16)
            product = dot(r8_t, shifted)
            even = pltpu.roll(product[:, :BLK], 1, 1, stride=1, stride_axis=0)
            odd = pltpu.roll(product[:, BLK:], 1, 1, stride=1, stride_axis=0)
            fbuf[2 * f] = jnp.sum(jnp.where(inside, previous, even), axis=0, keepdims=True)
            fbuf[2 * f + 1] = jnp.sum(jnp.where(inside, even, odd), axis=0, keepdims=True)
            return odd

        last = lax.fori_loop(0, PAIRS, lags, jnp.zeros((BLK, BLK), F32), unroll=2)
        fbuf[NB] = jnp.sum(jnp.where(inside, last, 0.0), axis=0, keepdims=True)

        for i in range(1, 4):
            other = lax.rem(part + i, 4)
            remote(
                fbuf.at[pl.ds(1 + QUART * other, QUART)], frecv.at[part],
                fr_send, fr_recv, 4 * plane + other,
            ).start()
        frecv[part] = fbuf[pl.ds(1 + QUART * part, QUART)]

        z = z_s[...].reshape(PAIRS * 8, 2 * BLK).astype(BF16)

        def convolve(d, carry):
            t0, t1, t2 = toep[2 * d], toep[2 * d + 1], toep[2 * d + 2]
            weights = jnp.concatenate(
                [jnp.concatenate([t1, t2], axis=1), jnp.concatenate([t0, t1], axis=1)], axis=0
            )
            y_s[pl.ds(d, PAIRS)] += dot(z, weights).reshape(PAIRS, 8, 2 * BLK)
            return carry

        lax.fori_loop(0, PAIRS, convolve, 0, unroll=2)

        wait_for(frecv.at[pl.ds(0, 3)], fr_recv)
        fq[...] = lag_scale * ((frecv[0] + frecv[1]) + (frecv[2] + frecv[3]))

        for half in range(2):
            y = y_s[:PAIRS, :, half * BLK : (half + 1) * BLK].reshape(PAIRS * 8, BLK)
            high = y.astype(BF16)
            rest = (y - high.astype(F32)).astype(BF16)
            yj_s[:, :, half * BLK : (half + 1) * BLK] = (
                dot(high, flip) + dot(rest, flip)
            ).reshape(PAIRS, 8, BLK)

        def spread_lags(i, carry):
            remote(fq, fgbuf.at[me], fb_send, fb_recv, lax.rem(me + i, NB)).start()
            return carry

        lax.fori_loop(1, NB, spread_lags, 0)
        fgbuf[me] = fq[...]

        def finish(b, y, yj, after, sums, skip_sum):
            p = pb_s[b]
            u = half_turn(jnp.where(low_rows, yj, y) + skip_col * p)
            short_tile = conv_s[b]
            he = jnp.concatenate([short_tile[8:] * u, short_tile[:8] * u], axis=0)
            x = recvb[b].astype(F32)
            total = tcol[0] * he
            new_sums = [sums[0] + he * x]
            turned = []
            for j in range(1, TAPS):
                t = pltpu.roll(he, BLK - j, 1)
                s = jnp.where(lane < BLK - j, t, after[j - 1])
                total = total + tcol[j] * s
                new_sums.append(sums[j] + s * x)
                turned.append(t)
            retb[b] = total.astype(BF16)
            return tuple(turned), tuple(new_sums), skip_sum + p * half_turn(p)

        def send_plane(zp):
            for b4 in range(4):
                b = 4 * zp + b4

                @pl.when(b != me)
                def _(b=b):
                    remote(retb.at[b], retr.at[me], ret_send, ret_recv, b).start()

        def post(i, carry):
            after, sums, skip_sum = carry
            zp = NB // 4 - 1 - i
            for b4 in range(3, -1, -1):
                y_half = slice(BLK, None) if b4 % 2 else slice(0, BLK)
                j_half = slice(0, BLK) if b4 % 2 else slice(BLK, None)
                e = 2 * zp + b4 // 2
                after, sums, skip_sum = finish(
                    4 * zp + b4, y_s[e, :, y_half], yj_s[PAIRS - 1 - e, :, j_half],
                    after, sums, skip_sum,
                )

            @pl.when(i > 0)
            def _():
                send_plane(zp + 1)

            return after, sums, skip_sum

        start = (
            empty,
            tuple(jnp.zeros((16, BLK), F32) for _ in range(TAPS)),
            jnp.zeros((8, BLK), F32),
        )
        _, sums, skip_sum = lax.fori_loop(0, NB // 4, post, start)

        line = jnp.zeros((16, BLK), F32)
        for j in range(TAPS):
            line = line + jnp.where(
                lane == 16 * j + row, jnp.sum(sums[j], axis=1, keepdims=True), 0.0
            )
        skip_line = jnp.where(
            lane[:8] == 16 * TAPS + row[:8], jnp.sum(skip_sum, axis=1, keepdims=True), 0.0
        )
        small[...] = tap_scale * (
            jnp.sum(line, axis=0, keepdims=True) + jnp.sum(skip_line, axis=0, keepdims=True)
        )
        send_plane(0)

        def spread_small(i, carry):
            remote(small, smallr.at[me], sm_send, sm_recv, lax.rem(me + i, NB)).start()
            return carry

        lax.fori_loop(1, NB, spread_small, 0)
        retr[me] = retb[me]
        smallr[me] = small[...]

    outs = [
        pltpu.make_async_copy(fgbuf, fg_hbm, out_sem.at[0]),
        pltpu.make_async_copy(retr, back_hbm, out_sem.at[1]),
        pltpu.make_async_copy(smallr, small_hbm, out_sem.at[2]),
    ]
    for out, buffer, sem in zip(outs, (fgbuf, retr, smallr), (fb_recv, ret_recv, sm_recv)):
        @pl.when(working)
        def _(buffer=buffer, sem=sem):
            wait_for(buffer.at[pl.ds(0, NW - 1)], sem)

        @pl.when(me >= NW)
        def _(buffer=buffer, sem=sem):
            wait_for(buffer, sem)

        out.start()

    @pl.when(working)
    def _drain():
        wait_for(sendb.at[pl.ds(0, NW - 1)], in_send)
        wait_for(frecv.at[pl.ds(0, 3)], fr_send)
        wait_for(retb.at[pl.ds(0, NB - 1)], ret_send)

        def drain(i, carry):
            wait_for(fq, fb_send)
            wait_for(small, sm_send)
            return carry

        lax.fori_loop(1, NB, drain, 0)

    @pl.when(me >= NW)
    def _():
        wait_for(sendb, in_send)

    for out in outs:
        out.wait()


def assemble(
    back_hbm, small_hbm, fg_hbm,
    out_ref, ig_ref, tapg_ref, skipg_ref, fg_ref,
    backb, smallb, fgbuf, sm_s, sems,
):
    loads = [
        pltpu.make_async_copy(back_hbm, backb, sems.at[0]),
        pltpu.make_async_copy(small_hbm, smallb, sems.at[1]),
        pltpu.make_async_copy(fg_hbm, fgbuf, sems.at[2]),
    ]
    for load in loads:
        load.start()
    perm = transposer()
    loads[0].wait()
    back = dot(backb[...].reshape(512, BLK), perm, ((0,), (0,))).astype(BF16)
    ig_ref[0] = back[:, 0:128]
    ig_ref[1] = back[:, 128:256]
    out_ref[...] = back[:, 256:384]
    ig_ref[2] = back[:, 384:512]

    loads[1].wait()
    sm_s[...] = jnp.zeros((BLK, BLK), F32)
    for m in range(NW):
        sm_s[m : m + 1, :] = smallb[m]
    select = jnp.where(iota((BLK, BLK), 0) == iota((BLK, BLK), 1) // 4, 1.0, 0.0)
    spread = lax.dot_general(
        sm_s[...].T, select, (((1,), (0,)), ((), ())),
        precision=lax.Precision.HIGHEST, preferred_element_type=F32,
    ).reshape(8, 16, BLK)
    row3 = iota((8, 16, BLK), 1)
    channel = iota((8, 16, BLK), 2) % 4
    for stream, first in enumerate((0, 4, 12)):
        picked = jnp.sum(jnp.where(row3 == channel + first, spread, 0.0), axis=1)
        tapg_ref[stream] = picked[:TAPS]
        if stream == 0:
            skipg_ref[...] = picked[TAPS:]

    loads[2].wait()
    for part in range(4):
        def lay(n, carry, part=part):
            at = pl.ds(pl.multiple_of((QUART * part + n) * BLK, BLK), BLK)
            for g in range(NG):
                fg_ref[g : g + 1, at] = fgbuf[4 * g + part, n]
            return carry

        lax.fori_loop(0, QUART, lay, 0)


def local(query_in, key_in, value_in, short_taps, long_filters, skip_gain, cotangent):
    vmem = pl.BlockSpec(memory_space=pltpu.VMEM)
    anywhere = pl.BlockSpec(memory_space=pl.ANY)
    dma = pltpu.SemaphoreType.DMA
    raw = (
        jax.ShapeDtypeStruct((NW, 16, BLK), BF16),
        jax.ShapeDtypeStruct((NW, 1, BLK), F32),
        jax.ShapeDtypeStruct((NW, QUART, 1, BLK), F32),
    )
    back, small, lag_rows = pl.pallas_call(
        kernel,
        out_shape=raw,
        in_specs=[anywhere] * 7,
        out_specs=(anywhere,) * 3,
        scratch_shapes=[
            pltpu.VMEM((4, BLK, BLK), BF16),
            pltpu.VMEM((3, TAPS, BLK), F32),
            pltpu.VMEM((NG, NB * BLK), BF16),
            pltpu.VMEM((1, BLK), F32),
            pltpu.VMEM((512, 512), BF16),
            pltpu.VMEM((NW, 16, BLK), BF16),
            pltpu.VMEM((NB, 16, BLK), BF16),
            pltpu.VMEM((NB + 1, BLK, BLK), BF16),
            pltpu.VMEM((TAPS + 1, 16, BLK), F32),
            pltpu.VMEM((NB, 16, BLK), F32),
            pltpu.VMEM((NB, 8, BLK), F32),
            pltpu.VMEM((32, 8, BLK), F32),
            pltpu.VMEM((PAIRS + 32, 8, 2 * BLK), F32),
            pltpu.VMEM((PAIRS, 8, 2 * BLK), F32),
            pltpu.VMEM((2 * PAIRS, 8, 2 * BLK), F32),
            pltpu.VMEM((PAIRS, 8, 2 * BLK), F32),
            pltpu.VMEM((NB, 16, BLK), BF16),
            pltpu.VMEM((NW, 16, BLK), BF16),
            pltpu.VMEM((1, BLK), F32),
            pltpu.VMEM((NW, 1, BLK), F32),
            pltpu.VMEM((NB + 1, 1, BLK), F32),
            pltpu.VMEM((4, QUART, 1, BLK), F32),
            pltpu.VMEM((QUART, 1, BLK), F32),
            pltpu.VMEM((NW, QUART, 1, BLK), F32),
            dma((7,)), dma((3,)), dma(()), dma((NB // 4,)), dma(()), dma(()), dma(()), dma(()),
            dma(()), dma(()), dma(()), dma(()),
        ],
        compiler_params=pltpu.CompilerParams(collective_id=0, has_side_effects=True),
        name="hyena",
    )(query_in, key_in, cotangent, value_in, short_taps, long_filters, skip_gain.reshape(1, BLK))
    block_out, input_grads, tap_grads, skip_grad, filter_grad = pl.pallas_call(
        assemble,
        out_shape=(
            jax.ShapeDtypeStruct((BLK, BLK), BF16),
            jax.ShapeDtypeStruct((3, BLK, BLK), BF16),
            jax.ShapeDtypeStruct((3, TAPS, BLK), F32),
            jax.ShapeDtypeStruct((1, BLK), F32),
            jax.ShapeDtypeStruct((NG, NB * BLK), F32),
        ),
        in_specs=[anywhere] * 3,
        out_specs=(vmem,) * 5,
        scratch_shapes=[
            pltpu.VMEM((NW, 16, BLK), BF16),
            pltpu.VMEM((NW, 1, BLK), F32),
            pltpu.VMEM((NW, QUART, 1, BLK), F32),
            pltpu.VMEM((BLK, BLK), F32),
            dma((3,)),
        ],
        name="assemble",
    )(back, small, lag_rows)
    return block_out, input_grads, tap_grads, skip_grad.reshape(BLK), filter_grad


def solution(mesh):
    in_specs = (
        P("seq", "chan"),
        P("seq", "chan"),
        P("seq", "chan"),
        P(None, None, "chan"),
        P("chan", None),
        P("chan"),
        P("seq", "chan"),
    )
    out_specs = (
        P("seq", "chan"),
        P(None, "seq", "chan"),
        P(None, None, "chan"),
        P("chan"),
        P("chan", None),
    )
    return jax.shard_map(local, mesh=mesh, in_specs=in_specs, out_specs=out_specs, check_vma=False)
```

```python
import math

import jax
import jax.numpy as jnp
from jax import lax
from jax.experimental import pallas as pl
from jax.experimental.pallas import tpu as pltpu
from jax.sharding import PartitionSpec as P

F32 = jnp.float32
BF16 = jnp.bfloat16
MESH = pl.DeviceIdType.MESH

BLK = 128
NB = 48
NW = 32
TAPS = 7
NG = 8
QUART = NB // 4
PAIRS = NB // 2


def iota(shape, dim):
    return lax.broadcasted_iota(jnp.int32, shape, dim)


def dot(a, b, dims=((1,), (0,))):
    return lax.dot_general(a, b, (dims, ((), ())), preferred_element_type=F32)


def half_turn(x):
    return pltpu.roll(x, 4, 0)


def remote(src, dst, send_sem, recv_sem, target):
    return pltpu.make_async_remote_copy(
        src_ref=src,
        dst_ref=dst,
        send_sem=send_sem,
        recv_sem=recv_sem,
        device_id={"seq": target},
        device_id_type=MESH,
    )


def wait_for(ref, sem):
    pltpu.make_async_copy(ref, ref, sem).wait()


def transposer():
    rho = iota((512, 1), 0)
    column = 128 * ((rho // 4) % 4) + 4 * (rho // 16) + rho % 4
    return jnp.where(iota((512, 512), 1) == column, 1.0, 0.0).astype(BF16)


def kernel(
    q_hbm, k_hbm, c_hbm, v_hbm, taps_hbm, filt_hbm, skip_hbm,
    back_hbm, small_hbm, fg_hbm,
    streams, taps_ref, filt_ref, skip_ref,
    perm, sendb, recvb, toep, tcol, conv_s, pb_s, r8_s, gg_s, ggb, z_s, zb, y_s, yj_s,
    retb, retr, small, smallr, fbuf, frecv, fq, fgbuf,
    load_sem, out_sem, in_send, in_recv, ret_send, ret_recv, sm_send, sm_recv,
    fr_send, fr_recv, fb_send, fb_recv, fx_send, fx_recv,
):
    me = lax.axis_index("seq")
    plane = me // 4
    part = me % 4
    tap_scale = 1.0 / math.sqrt(NB * BLK)
    lag_scale = 1.0 / math.sqrt(NB * BLK * 16)
    working = me < NW
    barrier = pltpu.get_barrier_semaphore()

    loads = [
        pltpu.make_async_copy(source, streams.at[r], load_sem.at[r])
        for r, source in enumerate((q_hbm, k_hbm, c_hbm, v_hbm))
    ]
    for load in loads:
        load.start()
    own_loads = [
        pltpu.make_async_copy(taps_hbm, taps_ref, load_sem.at[4]),
        pltpu.make_async_copy(filt_hbm, filt_ref, load_sem.at[5]),
        pltpu.make_async_copy(skip_hbm, skip_ref, load_sem.at[6]),
    ]

    @pl.when(working)
    def _greet():
        for load in own_loads:
            load.start()

        def greet(i, carry):
            pl.semaphore_signal(
                barrier, inc=1, device_id={"seq": lax.rem(me + i, NB)}, device_id_type=MESH
            )
            return carry

        lax.fori_loop(1, NB, greet, 0)

    perm[...] = transposer()
    for load in loads:
        load.wait()
    joined = jnp.concatenate([streams[r] for r in range(4)], axis=1)
    sendb[...] = dot(perm[...], joined, ((1,), (1,))).astype(BF16).reshape(NW, 16, BLK)

    lane = iota((16, BLK), 1)
    row = iota((16, BLK), 0)
    low_rows = iota((8, BLK), 0) < 4
    square_row = iota((BLK, BLK), 0)
    square_lane = iota((BLK, BLK), 1)
    identity = jnp.where(square_row == square_lane, 1.0, 0.0).astype(BF16)
    flip = jnp.where(square_row + square_lane == BLK - 1, 1.0, 0.0).astype(BF16)

    @pl.when(working)
    def _prepare():
        for load in own_loads:
            load.wait()

        own = lane == 4 * me + row % 4
        for j in range(TAPS):
            q_tap = jnp.broadcast_to(taps_ref[0, j : j + 1, :], (16, BLK))
            k_tap = jnp.broadcast_to(taps_ref[1, j : j + 1, :], (16, BLK))
            v_tap = jnp.broadcast_to(taps_ref[2, j : j + 1, :], (16, BLK))
            tap = jnp.where(row < 4, q_tap, jnp.where(row < 8, k_tap, v_tap))
            column = jnp.sum(jnp.where(own, tap, 0.0), axis=1, keepdims=True)
            column = jnp.broadcast_to(column, (16, BLK))
            unit = 1.0 if j == 0 else 0.0
            tcol[j] = jnp.where((row >= 8) & (row < 12), unit, column)
        skip_own = jnp.where(own, jnp.broadcast_to(skip_ref[...], (16, BLK)), 0.0)
        tcol[TAPS] = jnp.broadcast_to(jnp.sum(skip_own, axis=1, keepdims=True), (16, BLK))

        toep[0] = jnp.zeros((BLK, BLK), BF16)

        def build(n, previous):
            rows = filt_ref[:, pl.ds(pl.multiple_of(n * BLK, BLK), BLK)].astype(F32)
            line = jnp.sum(jnp.where(iota((NG, BLK), 0) == plane, rows, 0.0), axis=0, keepdims=True)
            turned = pltpu.roll(
                jnp.broadcast_to(line, (BLK, BLK)), 0, 1, stride=1, stride_axis=0
            )
            toep[n + 1] = jnp.where(square_lane >= square_row, turned, previous).astype(BF16)
            return turned

        lax.fori_loop(0, NB, build, jnp.zeros((BLK, BLK), F32), unroll=2)

        r8_s[PAIRS:] = jnp.zeros((32 - PAIRS, 8, BLK), F32)
        gg_s[PAIRS:] = jnp.zeros((42 - PAIRS, 8, 2 * BLK), F32)
        recvb[me] = sendb[me]
        pl.semaphore_wait(barrier, NW - 1)

    @pl.when(me >= NW)
    def _():
        pl.semaphore_wait(barrier, NW)

    for m in range(NW):
        @pl.when(m != me)
        def _(m=m):
            remote(sendb.at[m], recvb.at[me], in_send, in_recv.at[plane], m).start()

    @pl.when(working)
    def _work():
        skip_col = tcol[TAPS][:8]

        def short(z, carry):
            before, jm = carry

            @pl.when(z == plane)
            def _():
                wait_for(recvb.at[pl.ds(0, 3)], in_recv.at[z])

            @pl.when(z != plane)
            def _():
                wait_for(recvb.at[pl.ds(0, 4)], in_recv.at[z])

            for b4 in range(4):
                b = 4 * z + b4
                x = recvb[b].astype(F32)
                total = tcol[0] * x
                turned = []
                for j in range(1, TAPS):
                    t = pltpu.roll(x, j, 1)
                    total = total + tcol[j] * jnp.where(lane < j, before[j - 1], t)
                    turned.append(t)
                conv_s[b] = total
                pb_s[b] = (total[:8] * total[8:]).astype(BF16).astype(F32)
                before = tuple(turned)

            pb4 = pb_s[pl.ds(4 * z, 4)]
            pj4 = dot(pb4.reshape(32, BLK).astype(BF16), flip).reshape(4, 8, BLK)
            for half in range(2):
                e = 2 * z + half
                p0, p1 = pb4[2 * half], pb4[2 * half + 1]
                j0, j1 = pj4[2 * half], pj4[2 * half + 1]
                r8_s[PAIRS - 1 - e] = jnp.where(low_rows, p0, half_turn(p1))
                gg_s[PAIRS - 1 - e, :, :BLK] = jnp.where(low_rows, half_turn(j0), j1)
                gg_s[PAIRS - 1 - e, :, BLK:] = jnp.where(low_rows, half_turn(jm), j0)
                z_s[e, 4:, :BLK] = p0[4:]
                z_s[e, 4:, BLK:] = p1[4:]
                z_s[PAIRS - 1 - e, :4, :BLK] = j1[:4]
                z_s[PAIRS - 1 - e, :4, BLK:] = j0[:4]
                jm = j1
            return before, jm

        empty = tuple(jnp.zeros((16, BLK), F32) for _ in range(TAPS - 1))
        lax.fori_loop(0, NB // 4, short, (empty, jnp.zeros((8, BLK), F32)))

        r8_t = dot(identity, r8_s[...].reshape(256, BLK).astype(BF16), ((1,), (1,))).astype(BF16)
        inside = square_lane <= square_row

        for odd in range(2):
            ggb[odd] = gg_s[odd : odd + 40].reshape(320, 2 * BLK).astype(BF16)

        def fold(x):
            return jnp.sum(x.reshape(BLK // 8, 8, BLK), axis=0)

        within = None
        for f in range(PAIRS):
            depth = 256 if f < 8 else 128
            first = 8 * (f - f % 2)
            product = dot(r8_t[:, :depth], ggb[f % 2, first : first + depth, :])
            for half in range(2):
                n = 2 * f + half
                turned = pltpu.roll(
                    product[:, half * BLK : (half + 1) * BLK], 1, 1, stride=1, stride_axis=0
                )
                everything = fold(turned)
                next_within = fold(jnp.where(inside, turned, 0.0))
                if n > 0:
                    fbuf[n - 1] = jnp.sum(
                        within + (everything - next_within), axis=0, keepdims=True
                    )
                within = next_within
        fbuf[NB - 1] = jnp.sum(within, axis=0, keepdims=True)

        for i in range(1, 4):
            other = lax.rem(part + i, 4)
            remote(
                fbuf.at[pl.ds(QUART * other, QUART)], frecv.at[part],
                fr_send, fr_recv, 4 * plane + other,
            ).start()
        frecv[part] = fbuf[pl.ds(QUART * part, QUART)]

        zb[...] = z_s[...].reshape(PAIRS * 8, 2 * BLK).astype(BF16)
        for d in range(PAIRS):
            t0, t1, t2 = toep[2 * d], toep[2 * d + 1], toep[2 * d + 2]
            weights = jnp.concatenate(
                [jnp.concatenate([t1, t2], axis=1), jnp.concatenate([t0, t1], axis=1)], axis=0
            )
            term = dot(zb[: 8 * (PAIRS - d), :], weights).reshape(PAIRS - d, 8, 2 * BLK)
            if d == 0:
                y_s[...] = term
            else:
                y_s[d:] += term

        wait_for(frecv.at[pl.ds(0, 3)], fr_recv)
        fq[...] = lag_scale * ((frecv[0] + frecv[1]) + (frecv[2] + frecv[3]))

        for half in range(2):
            y = y_s[:, :, half * BLK : (half + 1) * BLK].reshape(PAIRS * 8, BLK)
            high = y.astype(BF16)
            rest = (y - high.astype(F32)).astype(BF16)
            yj_s[:, :, half * BLK : (half + 1) * BLK] = (
                dot(high, flip) + dot(rest, flip)
            ).reshape(PAIRS, 8, BLK)

        for zp in range(NB // 4):
            @pl.when(zp != plane)
            def _(zp=zp):
                remote(fq, fgbuf.at[part, plane], fb_send, fb_recv, 4 * zp + part).start()

        fgbuf[part, plane] = fq[...]

        def gates(b, y, yj):
            p = pb_s[b]
            u = half_turn(jnp.where(low_rows, yj, y) + skip_col * p)
            short_tile = conv_s[b]
            he = jnp.concatenate([short_tile[8:] * u, short_tile[:8] * u], axis=0)
            turned = tuple(pltpu.roll(he, BLK - j, 1) for j in range(1, TAPS))
            return he, turned, p * half_turn(p)

        def finish(he, turned, x, following, sums):
            total = tcol[0] * he
            new_sums = [sums[0] + he * x]
            for j in range(1, TAPS):
                s = jnp.where(lane < BLK - j, turned[j - 1], following[j - 1])
                total = total + tcol[j] * s
                new_sums.append(sums[j] + s * x)
            return total.astype(BF16), tuple(new_sums)

        def send_plane(zp):
            for b4 in range(4):
                b = 4 * zp + b4

                @pl.when(b != me)
                def _(b=b):
                    remote(retb.at[b + 1], retr.at[me], ret_send, ret_recv, b).start()

        def post(zp, carry):
            he, turned, x, sums, skip_sum = carry
            for b4 in range(4):
                b = 4 * zp + b4
                y_half = slice(BLK, None) if b4 % 2 else slice(0, BLK)
                j_half = slice(0, BLK) if b4 % 2 else slice(BLK, None)
                e = 2 * zp + b4 // 2
                new_he, following, skip_term = gates(
                    b, y_s[e, :, y_half], yj_s[PAIRS - 1 - e, :, j_half]
                )
                retb[b], sums = finish(he, turned, x, following, sums)
                he, turned, x = new_he, following, recvb[b].astype(F32)
                skip_sum = skip_sum + skip_term

            @pl.when((zp > 0) & (zp < 7))
            def _():
                send_plane(zp - 1)

            return he, turned, x, sums, skip_sum

        zero = jnp.zeros((16, BLK), F32)
        start = (zero, empty, zero, (zero,) * TAPS, jnp.zeros((8, BLK), F32))
        he, turned, x, sums, skip_sum = lax.fori_loop(0, NB // 4, post, start)
        retb[NB], sums = finish(he, turned, x, empty, sums)

        line = jnp.zeros((16, BLK), F32)
        for j in range(TAPS):
            line = line + jnp.where(
                lane == 16 * j + row, jnp.sum(sums[j], axis=1, keepdims=True), 0.0
            )
        skip_line = jnp.where(
            lane[:8] == 16 * TAPS + row[:8], jnp.sum(skip_sum, axis=1, keepdims=True), 0.0
        )
        small[...] = tap_scale * (
            jnp.sum(line, axis=0, keepdims=True) + jnp.sum(skip_line, axis=0, keepdims=True)
        )
        send_plane(6)

        def spread_small(i, carry):
            @pl.when(i != me)
            def _():
                remote(small, smallr.at[me], sm_send, sm_recv, i).start()

            return carry

        lax.fori_loop(0, NB // 2, spread_small, 0)
        for zp in range(7, NB // 4):
            send_plane(zp)
        lax.fori_loop(NB // 2, NB, spread_small, 0)
        retr[me] = retb[me + 1]
        smallr[me] = small[...]

    @pl.when(working)
    def _():
        wait_for(fgbuf.at[0, pl.ds(0, NG - 1)], fb_recv)

    @pl.when(me >= NW)
    def _():
        wait_for(fgbuf.at[0], fb_recv)

    for i in range(1, 4):
        other = lax.rem(part + i, 4)
        remote(fgbuf.at[part], fgbuf.at[part], fx_send, fx_recv, 4 * plane + other).start()

    outs = [
        pltpu.make_async_copy(retr, back_hbm, out_sem.at[0]),
        pltpu.make_async_copy(smallr, small_hbm, out_sem.at[1]),
        pltpu.make_async_copy(fgbuf, fg_hbm, out_sem.at[2]),
    ]
    for out, buffer, sem in zip(outs[:2], (retr, smallr), (ret_recv, sm_recv)):
        @pl.when(working)
        def _(buffer=buffer, sem=sem):
            wait_for(buffer.at[pl.ds(0, NW - 1)], sem)

        @pl.when(me >= NW)
        def _(buffer=buffer, sem=sem):
            wait_for(buffer, sem)

        out.start()
    wait_for(fgbuf.at[pl.ds(0, 3)], fx_recv)
    outs[2].start()

    @pl.when(working)
    def _drain():
        wait_for(sendb.at[pl.ds(0, NW - 1)], in_send)
        wait_for(frecv.at[pl.ds(0, 3)], fr_send)
        wait_for(retb.at[pl.ds(0, NB - 1)], ret_send)
        wait_for(fbuf.at[pl.ds(0, NB - 1)], sm_send)
        wait_for(fgbuf.at[0], fb_send)
        wait_for(fgbuf.at[0, pl.ds(0, 3)], fb_send)

    @pl.when(me >= NW)
    def _():
        wait_for(sendb, in_send)

    wait_for(fgbuf.at[pl.ds(0, 3)], fx_send)
    for out in outs:
        out.wait()


def assemble(
    back_hbm, small_hbm, fg_hbm,
    out_ref, ig_ref, tapg_ref, skipg_ref, fg_ref,
    backb, smallb, fgbuf, sm_s, sems,
):
    loads = [
        pltpu.make_async_copy(back_hbm, backb, sems.at[0]),
        pltpu.make_async_copy(small_hbm, smallb, sems.at[1]),
        pltpu.make_async_copy(fg_hbm, fgbuf, sems.at[2]),
    ]
    for load in loads:
        load.start()
    perm = transposer()
    loads[0].wait()
    back = dot(backb[...].reshape(512, BLK), perm, ((0,), (0,))).astype(BF16)
    ig_ref[0] = back[:, 0:128]
    ig_ref[1] = back[:, 128:256]
    out_ref[...] = back[:, 256:384]
    ig_ref[2] = back[:, 384:512]

    loads[1].wait()
    sm_s[...] = jnp.zeros((BLK, BLK), F32)
    for m in range(NW):
        sm_s[m : m + 1, :] = smallb[m]
    select = jnp.where(iota((BLK, BLK), 0) == iota((BLK, BLK), 1) // 4, 1.0, 0.0)
    spread = lax.dot_general(
        sm_s[...].T, select, (((1,), (0,)), ((), ())),
        precision=lax.Precision.HIGHEST, preferred_element_type=F32,
    ).reshape(8, 16, BLK)
    row3 = iota((8, 16, BLK), 1)
    channel = iota((8, 16, BLK), 2) % 4
    for stream, first in enumerate((0, 4, 12)):
        picked = jnp.sum(jnp.where(row3 == channel + first, spread, 0.0), axis=1)
        tapg_ref[stream] = picked[:TAPS]
        if stream == 0:
            skipg_ref[...] = picked[TAPS:]

    loads[2].wait()
    for part in range(4):
        def lay(n, carry, part=part):
            at = pl.ds(pl.multiple_of((QUART * part + n) * BLK, BLK), BLK)
            for g in range(NG):
                fg_ref[g : g + 1, at] = fgbuf[part, g, n]
            return carry

        lax.fori_loop(0, QUART, lay, 0)


def local(query_in, key_in, value_in, short_taps, long_filters, skip_gain, cotangent):
    vmem = pl.BlockSpec(memory_space=pltpu.VMEM)
    anywhere = pl.BlockSpec(memory_space=pl.ANY)
    dma = pltpu.SemaphoreType.DMA
    raw = (
        jax.ShapeDtypeStruct((NW, 16, BLK), BF16),
        jax.ShapeDtypeStruct((NW, 1, BLK), F32),
        jax.ShapeDtypeStruct((4, NG, QUART, 1, BLK), F32),
    )
    back, small, lag_rows = pl.pallas_call(
        kernel,
        out_shape=raw,
        in_specs=[anywhere] * 7,
        out_specs=(anywhere,) * 3,
        scratch_shapes=[
            pltpu.VMEM((4, BLK, BLK), BF16),
            pltpu.VMEM((3, TAPS, BLK), F32),
            pltpu.VMEM((NG, NB * BLK), BF16),
            pltpu.VMEM((1, BLK), F32),
            pltpu.VMEM((512, 512), BF16),
            pltpu.VMEM((NW, 16, BLK), BF16),
            pltpu.VMEM((NB, 16, BLK), BF16),
            pltpu.VMEM((NB + 1, BLK, BLK), BF16),
            pltpu.VMEM((TAPS + 1, 16, BLK), F32),
            pltpu.VMEM((NB, 16, BLK), F32),
            pltpu.VMEM((NB, 8, BLK), F32),
            pltpu.VMEM((32, 8, BLK), F32),
            pltpu.VMEM((42, 8, 2 * BLK), F32),
            pltpu.VMEM((2, 320, 2 * BLK), BF16),
            pltpu.VMEM((PAIRS, 8, 2 * BLK), F32),
            pltpu.VMEM((PAIRS * 8, 2 * BLK), BF16),
            pltpu.VMEM((PAIRS, 8, 2 * BLK), F32),
            pltpu.VMEM((PAIRS, 8, 2 * BLK), F32),
            pltpu.VMEM((NB + 1, 16, BLK), BF16),
            pltpu.VMEM((NW, 16, BLK), BF16),
            pltpu.VMEM((1, BLK), F32),
            pltpu.VMEM((NW, 1, BLK), F32),
            pltpu.VMEM((NB, 1, BLK), F32),
            pltpu.VMEM((4, QUART, 1, BLK), F32),
            pltpu.VMEM((QUART, 1, BLK), F32),
            pltpu.VMEM((4, NG, QUART, 1, BLK), F32),
            dma((7,)), dma((3,)), dma(()), dma((NB // 4,)), dma(()), dma(()), dma(()), dma(()),
            dma(()), dma(()), dma(()), dma(()), dma(()), dma(()),
        ],
        compiler_params=pltpu.CompilerParams(collective_id=0, has_side_effects=True),
        name="hyena",
    )(query_in, key_in, cotangent, value_in, short_taps, long_filters, skip_gain.reshape(1, BLK))
    block_out, input_grads, tap_grads, skip_grad, filter_grad = pl.pallas_call(
        assemble,
        out_shape=(
            jax.ShapeDtypeStruct((BLK, BLK), BF16),
            jax.ShapeDtypeStruct((3, BLK, BLK), BF16),
            jax.ShapeDtypeStruct((3, TAPS, BLK), F32),
            jax.ShapeDtypeStruct((1, BLK), F32),
            jax.ShapeDtypeStruct((NG, NB * BLK), F32),
        ),
        in_specs=[anywhere] * 3,
        out_specs=(vmem,) * 5,
        scratch_shapes=[
            pltpu.VMEM((NW, 16, BLK), BF16),
            pltpu.VMEM((NW, 1, BLK), F32),
            pltpu.VMEM((4, NG, QUART, 1, BLK), F32),
            pltpu.VMEM((BLK, BLK), F32),
            dma((3,)),
        ],
        name="assemble",
    )(back, small, lag_rows)
    return block_out, input_grads, tap_grads, skip_grad.reshape(BLK), filter_grad


def solution(mesh):
    in_specs = (
        P("seq", "chan"),
        P("seq", "chan"),
        P("seq", "chan"),
        P(None, None, "chan"),
        P("chan", None),
        P("chan"),
        P("seq", "chan"),
    )
    out_specs = (
        P("seq", "chan"),
        P(None, "seq", "chan"),
        P(None, None, "chan"),
        P("chan"),
        P("chan", None),
    )
    return jax.shard_map(local, mesh=mesh, in_specs=in_specs, out_specs=out_specs, check_vma=False)
```

```python
import math

import jax
import jax.numpy as jnp
from jax import lax
from jax.experimental import pallas as pl
from jax.experimental.pallas import tpu as pltpu
from jax.sharding import PartitionSpec as P

F32 = jnp.float32
BF16 = jnp.bfloat16
MESH = pl.DeviceIdType.MESH

BLK = 128
NB = 48
NW = 32
TAPS = 7
NG = 8
QUART = NB // 4
PAIRS = NB // 2


def iota(shape, dim):
    return lax.broadcasted_iota(jnp.int32, shape, dim)


def dot(a, b, dims=((1,), (0,))):
    return lax.dot_general(a, b, (dims, ((), ())), preferred_element_type=F32)


def half_turn(x):
    return pltpu.roll(x, 4, 0)


def remote(src, dst, send_sem, recv_sem, target):
    return pltpu.make_async_remote_copy(
        src_ref=src,
        dst_ref=dst,
        send_sem=send_sem,
        recv_sem=recv_sem,
        device_id={"seq": target},
        device_id_type=MESH,
    )


def wait_for(ref, sem):
    pltpu.make_async_copy(ref, ref, sem).wait()


def transposer():
    rho = iota((512, 1), 0)
    column = 128 * ((rho // 4) % 4) + 4 * (rho // 16) + rho % 4
    return jnp.where(iota((512, 512), 1) == column, 1.0, 0.0).astype(BF16)


def kernel(
    q_hbm, k_hbm, c_hbm, v_hbm, taps_hbm, filt_hbm, skip_hbm,
    back_hbm, small_hbm, fg_hbm,
    streams, taps_ref, filt_ref, skip_ref,
    perm, sendb, recvb, toep, tcol, conv_s, pb_s, r8_s, gg_s, ggb, z_s, zb, y_s, yj_s,
    retb, retr, small, smallr, fbuf, frecv, fq, fgbuf,
    load_sem, out_sem, in_send, in_recv, ret_send, ret_recv, sm_send, sm_recv,
    fr_send, fr_recv, fb_send, fb_recv, fx_send, fx_recv, ready,
):
    me = lax.axis_index("seq")
    plane = me // 4
    part = me % 4
    tap_scale = 1.0 / math.sqrt(NB * BLK)
    lag_scale = 1.0 / math.sqrt(NB * BLK * 16)
    working = me < NW
    barrier = pltpu.get_barrier_semaphore()

    loads = [
        pltpu.make_async_copy(source, streams.at[r], load_sem.at[r])
        for r, source in enumerate((q_hbm, k_hbm, c_hbm, v_hbm))
    ]
    for load in loads:
        load.start()
    own_loads = [
        pltpu.make_async_copy(taps_hbm, taps_ref, load_sem.at[4]),
        pltpu.make_async_copy(filt_hbm, filt_ref, load_sem.at[5]),
        pltpu.make_async_copy(skip_hbm, skip_ref, load_sem.at[6]),
    ]

    @pl.when(working)
    def _greet():
        for load in own_loads:
            load.start()

        def greet(i, carry):
            @pl.when(i != me)
            def _():
                pl.semaphore_signal(barrier, inc=1, device_id={"seq": i}, device_id_type=MESH)

            return carry

        lax.fori_loop(4 * plane, NB, greet, 0)

    perm[...] = transposer()
    for load in loads:
        load.wait()
    joined = jnp.concatenate([streams[r] for r in range(4)], axis=1)
    sendb[...] = dot(perm[...], joined, ((1,), (1,))).astype(BF16).reshape(NW, 16, BLK)

    lane = iota((16, BLK), 1)
    row = iota((16, BLK), 0)
    low_rows = iota((8, BLK), 0) < 4
    square_row = iota((BLK, BLK), 0)
    square_lane = iota((BLK, BLK), 1)
    identity = jnp.where(square_row == square_lane, 1.0, 0.0).astype(BF16)
    flip = jnp.where(square_row + square_lane == BLK - 1, 1.0, 0.0).astype(BF16)

    def send_in(zp):
        for m in range(4 * zp, 4 * zp + 4):
            @pl.when(m != me)
            def _(m=m):
                remote(sendb.at[m], recvb.at[me], in_send, in_recv.at[plane], m).start()

    @pl.when(working)
    def _():
        pl.semaphore_wait(barrier, 4 * plane + 3)

        def tell(i, carry):
            pl.semaphore_signal(
                ready.at[plane], inc=1, device_id={"seq": i}, device_id_type=MESH
            )
            return carry

        lax.fori_loop(0, 4 * plane, tell, 0)

    @pl.when(me >= NW)
    def _():
        pl.semaphore_wait(barrier, NW)

    for zp in range(NW // 4):
        @pl.when(zp <= plane)
        def _(zp=zp):
            send_in(zp)

    @pl.when(working)
    def _prepare():
        for load in own_loads:
            load.wait()

        own = lane == 4 * me + row % 4
        for j in range(TAPS):
            q_tap = jnp.broadcast_to(taps_ref[0, j : j + 1, :], (16, BLK))
            k_tap = jnp.broadcast_to(taps_ref[1, j : j + 1, :], (16, BLK))
            v_tap = jnp.broadcast_to(taps_ref[2, j : j + 1, :], (16, BLK))
            tap = jnp.where(row < 4, q_tap, jnp.where(row < 8, k_tap, v_tap))
            column = jnp.sum(jnp.where(own, tap, 0.0), axis=1, keepdims=True)
            column = jnp.broadcast_to(column, (16, BLK))
            unit = 1.0 if j == 0 else 0.0
            tcol[j] = jnp.where((row >= 8) & (row < 12), unit, column)
        skip_own = jnp.where(own, jnp.broadcast_to(skip_ref[...], (16, BLK)), 0.0)
        tcol[TAPS] = jnp.broadcast_to(jnp.sum(skip_own, axis=1, keepdims=True), (16, BLK))

        toep[0] = jnp.zeros((BLK, BLK), BF16)

        def build(n, previous):
            rows = filt_ref[:, pl.ds(pl.multiple_of(n * BLK, BLK), BLK)].astype(F32)
            line = jnp.sum(jnp.where(iota((NG, BLK), 0) == plane, rows, 0.0), axis=0, keepdims=True)
            turned = pltpu.roll(
                jnp.broadcast_to(line, (BLK, BLK)), 0, 1, stride=1, stride_axis=0
            )
            toep[n + 1] = jnp.where(square_lane >= square_row, turned, previous).astype(BF16)
            return turned

        lax.fori_loop(0, NB, build, jnp.zeros((BLK, BLK), F32), unroll=2)

        r8_s[PAIRS:] = jnp.zeros((32 - PAIRS, 8, BLK), F32)
        gg_s[PAIRS:] = jnp.zeros((42 - PAIRS, 8, 2 * BLK), F32)
        recvb[me] = sendb[me]

    for zp in range(1, NW // 4):
        @pl.when(zp > plane)
        def _(zp=zp):
            pl.semaphore_wait(ready.at[zp], 4)
            send_in(zp)

    @pl.when(working)
    def _work():
        skip_col = tcol[TAPS][:8]

        def short(z, carry):
            before, jm = carry

            @pl.when(z == plane)
            def _():
                wait_for(recvb.at[pl.ds(0, 3)], in_recv.at[z])

            @pl.when(z != plane)
            def _():
                wait_for(recvb.at[pl.ds(0, 4)], in_recv.at[z])

            for b4 in range(4):
                b = 4 * z + b4
                x = recvb[b].astype(F32)
                total = tcol[0] * x
                turned = []
                for j in range(1, TAPS):
                    t = pltpu.roll(x, j, 1)
                    total = total + tcol[j] * jnp.where(lane < j, before[j - 1], t)
                    turned.append(t)
                conv_s[b] = total
                pb_s[b] = (total[:8] * total[8:]).astype(BF16).astype(F32)
                before = tuple(turned)

            pb4 = pb_s[pl.ds(4 * z, 4)]
            pj4 = dot(pb4.reshape(32, BLK).astype(BF16), flip).reshape(4, 8, BLK)
            for half in range(2):
                e = 2 * z + half
                p0, p1 = pb4[2 * half], pb4[2 * half + 1]
                j0, j1 = pj4[2 * half], pj4[2 * half + 1]
                r8_s[PAIRS - 1 - e] = jnp.where(low_rows, p0, half_turn(p1))
                gg_s[PAIRS - 1 - e, :, :BLK] = jnp.where(low_rows, half_turn(j0), j1)
                gg_s[PAIRS - 1 - e, :, BLK:] = jnp.where(low_rows, half_turn(jm), j0)
                z_s[e, 4:, :BLK] = p0[4:]
                z_s[e, 4:, BLK:] = p1[4:]
                z_s[PAIRS - 1 - e, :4, :BLK] = j1[:4]
                z_s[PAIRS - 1 - e, :4, BLK:] = j0[:4]
                jm = j1
            return before, jm

        empty = tuple(jnp.zeros((16, BLK), F32) for _ in range(TAPS - 1))
        lax.fori_loop(0, NB // 4, short, (empty, jnp.zeros((8, BLK), F32)))

        r8_t = dot(identity, r8_s[...].reshape(256, BLK).astype(BF16), ((1,), (1,))).astype(BF16)
        inside = square_lane <= square_row

        for odd in range(2):
            ggb[odd] = gg_s[odd : odd + 40].reshape(320, 2 * BLK).astype(BF16)

        def fold(x):
            return jnp.sum(x.reshape(BLK // 8, 8, BLK), axis=0)

        within = None
        for f in range(PAIRS):
            depth = 256 if f < 8 else 128
            first = 8 * (f - f % 2)
            product = dot(r8_t[:, :depth], ggb[f % 2, first : first + depth, :])
            for half in range(2):
                n = 2 * f + half
                turned = pltpu.roll(
                    product[:, half * BLK : (half + 1) * BLK], 1, 1, stride=1, stride_axis=0
                )
                everything = fold(turned)
                next_within = fold(jnp.where(inside, turned, 0.0))
                if n > 0:
                    fbuf[n - 1] = jnp.sum(
                        within + (everything - next_within), axis=0, keepdims=True
                    )
                within = next_within
        fbuf[NB - 1] = jnp.sum(within, axis=0, keepdims=True)

        for i in range(1, 4):
            other = lax.rem(part + i, 4)
            remote(
                fbuf.at[pl.ds(QUART * other, QUART)], frecv.at[part],
                fr_send, fr_recv, 4 * plane + other,
            ).start()
        frecv[part] = fbuf[pl.ds(QUART * part, QUART)]

        zb[...] = z_s[...].reshape(PAIRS * 8, 2 * BLK).astype(BF16)
        for d in range(PAIRS):
            t0, t1, t2 = toep[2 * d], toep[2 * d + 1], toep[2 * d + 2]
            weights = jnp.concatenate(
                [jnp.concatenate([t1, t2], axis=1), jnp.concatenate([t0, t1], axis=1)], axis=0
            )
            term = dot(zb[: 8 * (PAIRS - d), :], weights).reshape(PAIRS - d, 8, 2 * BLK)
            if d == 0:
                y_s[...] = term
            else:
                y_s[d:] += term

        wait_for(frecv.at[pl.ds(0, 3)], fr_recv)
        fq[...] = lag_scale * ((frecv[0] + frecv[1]) + (frecv[2] + frecv[3]))

        for half in range(2):
            y = y_s[:, :, half * BLK : (half + 1) * BLK].reshape(PAIRS * 8, BLK)
            high = y.astype(BF16)
            rest = (y - high.astype(F32)).astype(BF16)
            yj_s[:, :, half * BLK : (half + 1) * BLK] = (
                dot(high, flip) + dot(rest, flip)
            ).reshape(PAIRS, 8, BLK)

        for zp in range(NB // 4):
            @pl.when(zp != plane)
            def _(zp=zp):
                remote(fq, fgbuf.at[part, plane], fb_send, fb_recv, 4 * zp + part).start()

        fgbuf[part, plane] = fq[...]

        def gates(b, y, yj):
            p = pb_s[b]
            u = half_turn(jnp.where(low_rows, yj, y) + skip_col * p)
            short_tile = conv_s[b]
            he = jnp.concatenate([short_tile[8:] * u, short_tile[:8] * u], axis=0)
            turned = tuple(pltpu.roll(he, BLK - j, 1) for j in range(1, TAPS))
            return he, turned, p * half_turn(p)

        def finish(he, turned, x, following, sums):
            total = tcol[0] * he
            new_sums = [sums[0] + he * x]
            for j in range(1, TAPS):
                s = jnp.where(lane < BLK - j, turned[j - 1], following[j - 1])
                total = total + tcol[j] * s
                new_sums.append(sums[j] + s * x)
            return total.astype(BF16), tuple(new_sums)

        def send_plane(zp):
            for b4 in range(4):
                b = 4 * zp + b4

                @pl.when(b != me)
                def _(b=b):
                    remote(retb.at[b + 1], retr.at[me], ret_send, ret_recv, b).start()

        def post(zp, carry):
            he, turned, x, sums, skip_sum = carry
            for b4 in range(4):
                b = 4 * zp + b4
                y_half = slice(BLK, None) if b4 % 2 else slice(0, BLK)
                j_half = slice(0, BLK) if b4 % 2 else slice(BLK, None)
                e = 2 * zp + b4 // 2
                new_he, following, skip_term = gates(
                    b, y_s[e, :, y_half], yj_s[PAIRS - 1 - e, :, j_half]
                )
                retb[b], sums = finish(he, turned, x, following, sums)
                he, turned, x = new_he, following, recvb[b].astype(F32)
                skip_sum = skip_sum + skip_term

            @pl.when((zp > 0) & (zp < 7))
            def _():
                send_plane(zp - 1)

            return he, turned, x, sums, skip_sum

        zero = jnp.zeros((16, BLK), F32)
        start = (zero, empty, zero, (zero,) * TAPS, jnp.zeros((8, BLK), F32))
        he, turned, x, sums, skip_sum = lax.fori_loop(0, NB // 4, post, start)
        retb[NB], sums = finish(he, turned, x, empty, sums)

        line = jnp.zeros((16, BLK), F32)
        for j in range(TAPS):
            line = line + jnp.where(
                lane == 16 * j + row, jnp.sum(sums[j], axis=1, keepdims=True), 0.0
            )
        skip_line = jnp.where(
            lane[:8] == 16 * TAPS + row[:8], jnp.sum(skip_sum, axis=1, keepdims=True), 0.0
        )
        small[...] = tap_scale * (
            jnp.sum(line, axis=0, keepdims=True) + jnp.sum(skip_line, axis=0, keepdims=True)
        )
        send_plane(6)

        def spread_small(i, carry):
            @pl.when(i != me)
            def _():
                remote(small, smallr.at[me], sm_send, sm_recv, i).start()

            return carry

        lax.fori_loop(0, NB // 2, spread_small, 0)
        for zp in range(7, NB // 4):
            send_plane(zp)
        lax.fori_loop(NB // 2, NB, spread_small, 0)
        retr[me] = retb[me + 1]
        smallr[me] = small[...]

    @pl.when(working)
    def _():
        wait_for(fgbuf.at[0, pl.ds(0, NG - 1)], fb_recv)

    @pl.when(me >= NW)
    def _():
        wait_for(fgbuf.at[0], fb_recv)

    for i in range(1, 4):
        other = lax.rem(part + i, 4)
        remote(fgbuf.at[part], fgbuf.at[part], fx_send, fx_recv, 4 * plane + other).start()

    outs = [
        pltpu.make_async_copy(retr, back_hbm, out_sem.at[0]),
        pltpu.make_async_copy(smallr, small_hbm, out_sem.at[1]),
        pltpu.make_async_copy(fgbuf, fg_hbm, out_sem.at[2]),
    ]
    for out, buffer, sem in zip(outs[:2], (retr, smallr), (ret_recv, sm_recv)):
        @pl.when(working)
        def _(buffer=buffer, sem=sem):
            wait_for(buffer.at[pl.ds(0, NW - 1)], sem)

        @pl.when(me >= NW)
        def _(buffer=buffer, sem=sem):
            wait_for(buffer, sem)

        out.start()
    wait_for(fgbuf.at[pl.ds(0, 3)], fx_recv)
    outs[2].start()

    @pl.when(working)
    def _drain():
        wait_for(sendb.at[pl.ds(0, NW - 1)], in_send)
        wait_for(frecv.at[pl.ds(0, 3)], fr_send)
        wait_for(retb.at[pl.ds(0, NB - 1)], ret_send)
        wait_for(fbuf.at[pl.ds(0, NB - 1)], sm_send)
        wait_for(fgbuf.at[0], fb_send)
        wait_for(fgbuf.at[0, pl.ds(0, 3)], fb_send)

    @pl.when(me >= NW)
    def _():
        wait_for(sendb, in_send)

    wait_for(fgbuf.at[pl.ds(0, 3)], fx_send)
    for out in outs:
        out.wait()


def assemble(
    back_hbm, small_hbm, fg_hbm,
    out_ref, ig_ref, tapg_ref, skipg_ref, fg_ref,
    backb, smallb, fgbuf, sm_s, sems,
):
    loads = [
        pltpu.make_async_copy(back_hbm, backb, sems.at[0]),
        pltpu.make_async_copy(small_hbm, smallb, sems.at[1]),
        pltpu.make_async_copy(fg_hbm, fgbuf, sems.at[2]),
    ]
    for load in loads:
        load.start()
    perm = transposer()
    loads[0].wait()
    back = dot(backb[...].reshape(512, BLK), perm, ((0,), (0,))).astype(BF16)
    ig_ref[0] = back[:, 0:128]
    ig_ref[1] = back[:, 128:256]
    out_ref[...] = back[:, 256:384]
    ig_ref[2] = back[:, 384:512]

    loads[1].wait()
    sm_s[...] = jnp.zeros((BLK, BLK), F32)
    for m in range(NW):
        sm_s[m : m + 1, :] = smallb[m]
    select = jnp.where(iota((BLK, BLK), 0) == iota((BLK, BLK), 1) // 4, 1.0, 0.0)
    spread = lax.dot_general(
        sm_s[...].T, select, (((1,), (0,)), ((), ())),
        precision=lax.Precision.HIGHEST, preferred_element_type=F32,
    ).reshape(8, 16, BLK)
    row3 = iota((8, 16, BLK), 1)
    channel = iota((8, 16, BLK), 2) % 4
    for stream, first in enumerate((0, 4, 12)):
        picked = jnp.sum(jnp.where(row3 == channel + first, spread, 0.0), axis=1)
        tapg_ref[stream] = picked[:TAPS]
        if stream == 0:
            skipg_ref[...] = picked[TAPS:]

    loads[2].wait()
    for part in range(4):
        def lay(n, carry, part=part):
            at = pl.ds(pl.multiple_of((QUART * part + n) * BLK, BLK), BLK)
            for g in range(NG):
                fg_ref[g : g + 1, at] = fgbuf[part, g, n]
            return carry

        lax.fori_loop(0, QUART, lay, 0)


def local(query_in, key_in, value_in, short_taps, long_filters, skip_gain, cotangent):
    vmem = pl.BlockSpec(memory_space=pltpu.VMEM)
    anywhere = pl.BlockSpec(memory_space=pl.ANY)
    dma = pltpu.SemaphoreType.DMA
    raw = (
        jax.ShapeDtypeStruct((NW, 16, BLK), BF16),
        jax.ShapeDtypeStruct((NW, 1, BLK), F32),
        jax.ShapeDtypeStruct((4, NG, QUART, 1, BLK), F32),
    )
    back, small, lag_rows = pl.pallas_call(
        kernel,
        out_shape=raw,
        in_specs=[anywhere] * 7,
        out_specs=(anywhere,) * 3,
        scratch_shapes=[
            pltpu.VMEM((4, BLK, BLK), BF16),
            pltpu.VMEM((3, TAPS, BLK), F32),
            pltpu.VMEM((NG, NB * BLK), BF16),
            pltpu.VMEM((1, BLK), F32),
            pltpu.VMEM((512, 512), BF16),
            pltpu.VMEM((NW, 16, BLK), BF16),
            pltpu.VMEM((NB, 16, BLK), BF16),
            pltpu.VMEM((NB + 1, BLK, BLK), BF16),
            pltpu.VMEM((TAPS + 1, 16, BLK), F32),
            pltpu.VMEM((NB, 16, BLK), F32),
            pltpu.VMEM((NB, 8, BLK), F32),
            pltpu.VMEM((32, 8, BLK), F32),
            pltpu.VMEM((42, 8, 2 * BLK), F32),
            pltpu.VMEM((2, 320, 2 * BLK), BF16),
            pltpu.VMEM((PAIRS, 8, 2 * BLK), F32),
            pltpu.VMEM((PAIRS * 8, 2 * BLK), BF16),
            pltpu.VMEM((PAIRS, 8, 2 * BLK), F32),
            pltpu.VMEM((PAIRS, 8, 2 * BLK), F32),
            pltpu.VMEM((NB + 1, 16, BLK), BF16),
            pltpu.VMEM((NW, 16, BLK), BF16),
            pltpu.VMEM((1, BLK), F32),
            pltpu.VMEM((NW, 1, BLK), F32),
            pltpu.VMEM((NB, 1, BLK), F32),
            pltpu.VMEM((4, QUART, 1, BLK), F32),
            pltpu.VMEM((QUART, 1, BLK), F32),
            pltpu.VMEM((4, NG, QUART, 1, BLK), F32),
            dma((7,)), dma((3,)), dma(()), dma((NB // 4,)), dma(()), dma(()), dma(()), dma(()),
            dma(()), dma(()), dma(()), dma(()), dma(()), dma(()),
            pltpu.SemaphoreType.REGULAR((NW // 4,)),
        ],
        compiler_params=pltpu.CompilerParams(collective_id=0, has_side_effects=True),
        name="hyena",
    )(query_in, key_in, cotangent, value_in, short_taps, long_filters, skip_gain.reshape(1, BLK))
    block_out, input_grads, tap_grads, skip_grad, filter_grad = pl.pallas_call(
        assemble,
        out_shape=(
            jax.ShapeDtypeStruct((BLK, BLK), BF16),
            jax.ShapeDtypeStruct((3, BLK, BLK), BF16),
            jax.ShapeDtypeStruct((3, TAPS, BLK), F32),
            jax.ShapeDtypeStruct((1, BLK), F32),
            jax.ShapeDtypeStruct((NG, NB * BLK), F32),
        ),
        in_specs=[anywhere] * 3,
        out_specs=(vmem,) * 5,
        scratch_shapes=[
            pltpu.VMEM((NW, 16, BLK), BF16),
            pltpu.VMEM((NW, 1, BLK), F32),
            pltpu.VMEM((4, NG, QUART, 1, BLK), F32),
            pltpu.VMEM((BLK, BLK), F32),
            dma((3,)),
        ],
        name="assemble",
    )(back, small, lag_rows)
    return block_out, input_grads, tap_grads, skip_grad.reshape(BLK), filter_grad


def solution(mesh):
    in_specs = (
        P("seq", "chan"),
        P("seq", "chan"),
        P("seq", "chan"),
        P(None, None, "chan"),
        P("chan", None),
        P("chan"),
        P("seq", "chan"),
    )
    out_specs = (
        P("seq", "chan"),
        P(None, "seq", "chan"),
        P(None, None, "chan"),
        P("chan"),
        P("chan", None),
    )
    return jax.shard_map(local, mesh=mesh, in_specs=in_specs, out_specs=out_specs, check_vma=False)
```

```python
import math

import jax
import jax.numpy as jnp
from jax import lax
from jax.experimental import pallas as pl
from jax.experimental.pallas import tpu as pltpu
from jax.sharding import PartitionSpec as P

F32 = jnp.float32
BF16 = jnp.bfloat16
MESH = pl.DeviceIdType.MESH

BLK = 128
NB = 48
NW = 32
TAPS = 7
NG = 8
QUART = NB // 4
PAIRS = NB // 2


def iota(shape, dim):
    return lax.broadcasted_iota(jnp.int32, shape, dim)


def dot(a, b, dims=((1,), (0,))):
    return lax.dot_general(a, b, (dims, ((), ())), preferred_element_type=F32)


def half_turn(x):
    return pltpu.roll(x, 4, 0)


def remote(src, dst, send_sem, recv_sem, target):
    return pltpu.make_async_remote_copy(
        src_ref=src,
        dst_ref=dst,
        send_sem=send_sem,
        recv_sem=recv_sem,
        device_id={"seq": target},
        device_id_type=MESH,
    )


def wait_for(ref, sem):
    pltpu.make_async_copy(ref, ref, sem).wait()


def transposer():
    rho = iota((512, 1), 0)
    column = 128 * ((rho // 4) % 4) + 4 * (rho // 16) + rho % 4
    return jnp.where(iota((512, 512), 1) == column, 1.0, 0.0).astype(BF16)


def kernel(
    q_hbm, k_hbm, c_hbm, v_hbm, taps_hbm, filt_hbm, skip_hbm,
    back_hbm, small_hbm, fg_hbm,
    streams, taps_ref, filt_ref, skip_ref,
    perm, sendb, recvb, toep, tcol, conv_s, pb_s, r8_s, gg_s, ggb, z_s, zb, y_s, yj_s,
    retb, retr, small, smallr, fbuf, frecv, fqf, fq, fgbuf,
    load_sem, out_sem, in_send, in_recv, ret_send, ret_recv, sm_send, sm_recv,
    fr_send, fr_recv, fb_send, fb_recv, fx_send, fx_recv, ready,
):
    me = lax.axis_index("seq")
    plane = me // 4
    part = me % 4
    tap_scale = 1.0 / math.sqrt(NB * BLK)
    lag_scale = 1.0 / math.sqrt(NB * BLK * 16)
    working = me < NW
    barrier = pltpu.get_barrier_semaphore()

    loads = [
        pltpu.make_async_copy(source, streams.at[r], load_sem.at[r])
        for r, source in enumerate((q_hbm, k_hbm, c_hbm, v_hbm))
    ]
    for load in loads:
        load.start()
    own_loads = [
        pltpu.make_async_copy(taps_hbm, taps_ref, load_sem.at[4]),
        pltpu.make_async_copy(filt_hbm, filt_ref, load_sem.at[5]),
        pltpu.make_async_copy(skip_hbm, skip_ref, load_sem.at[6]),
    ]

    @pl.when(working)
    def _greet():
        for load in own_loads:
            load.start()

        def greet(i, carry):
            @pl.when(i != me)
            def _():
                pl.semaphore_signal(barrier, inc=1, device_id={"seq": i}, device_id_type=MESH)

            return carry

        lax.fori_loop(4 * plane, NB, greet, 0)

    perm[...] = transposer()
    for load in loads:
        load.wait()
    joined = jnp.concatenate([streams[r] for r in range(4)], axis=1)
    sendb[...] = dot(perm[...], joined, ((1,), (1,))).astype(BF16).reshape(NW, 16, BLK)

    lane = iota((16, BLK), 1)
    row = iota((16, BLK), 0)
    low_rows = iota((8, BLK), 0) < 4
    square_row = iota((BLK, BLK), 0)
    square_lane = iota((BLK, BLK), 1)
    identity = jnp.where(square_row == square_lane, 1.0, 0.0).astype(BF16)
    flip = jnp.where(square_row + square_lane == BLK - 1, 1.0, 0.0).astype(BF16)

    def send_in(zp):
        for m in range(4 * zp, 4 * zp + 4):
            @pl.when(m != me)
            def _(m=m):
                remote(sendb.at[m], recvb.at[me], in_send, in_recv.at[plane], m).start()

    @pl.when(working)
    def _():
        pl.semaphore_wait(barrier, 4 * plane + 3)

        def tell(i, carry):
            pl.semaphore_signal(
                ready.at[plane], inc=1, device_id={"seq": i}, device_id_type=MESH
            )
            return carry

        lax.fori_loop(0, 4 * plane, tell, 0)

    @pl.when(me >= NW)
    def _():
        pl.semaphore_wait(barrier, NW)

    for zp in range(NW // 4):
        @pl.when(zp <= plane)
        def _(zp=zp):
            send_in(zp)

    @pl.when(working)
    def _prepare():
        for load in own_loads:
            load.wait()

        own = lane == 4 * me + row % 4
        for j in range(TAPS):
            q_tap = jnp.broadcast_to(taps_ref[0, j : j + 1, :], (16, BLK))
            k_tap = jnp.broadcast_to(taps_ref[1, j : j + 1, :], (16, BLK))
            v_tap = jnp.broadcast_to(taps_ref[2, j : j + 1, :], (16, BLK))
            tap = jnp.where(row < 4, q_tap, jnp.where(row < 8, k_tap, v_tap))
            column = jnp.sum(jnp.where(own, tap, 0.0), axis=1, keepdims=True)
            column = jnp.broadcast_to(column, (16, BLK))
            unit = 1.0 if j == 0 else 0.0
            tcol[j] = jnp.where((row >= 8) & (row < 12), unit, column)
        skip_own = jnp.where(own, jnp.broadcast_to(skip_ref[...], (16, BLK)), 0.0)
        tcol[TAPS] = jnp.broadcast_to(jnp.sum(skip_own, axis=1, keepdims=True), (16, BLK))

        toep[0] = jnp.zeros((BLK, BLK), BF16)

        def build(n, previous):
            rows = filt_ref[:, pl.ds(pl.multiple_of(n * BLK, BLK), BLK)].astype(F32)
            line = jnp.sum(jnp.where(iota((NG, BLK), 0) == plane, rows, 0.0), axis=0, keepdims=True)
            turned = pltpu.roll(
                jnp.broadcast_to(line, (BLK, BLK)), 0, 1, stride=1, stride_axis=0
            )
            toep[n + 1] = jnp.where(square_lane >= square_row, turned, previous).astype(BF16)
            return turned

        lax.fori_loop(0, NB, build, jnp.zeros((BLK, BLK), F32), unroll=2)

        r8_s[PAIRS:] = jnp.zeros((32 - PAIRS, 8, BLK), F32)
        gg_s[PAIRS:] = jnp.zeros((42 - PAIRS, 8, 2 * BLK), F32)
        recvb[me] = sendb[me]

    for zp in range(1, NW // 4):
        @pl.when(zp > plane)
        def _(zp=zp):
            pl.semaphore_wait(ready.at[zp], 4)
            send_in(zp)

    def forward_lags():
        for i in range(1, 4):
            other = lax.rem(part + i, 4)
            remote(fgbuf.at[part], fgbuf.at[part], fx_send, fx_recv, 4 * plane + other).start()

    @pl.when(working)
    def _work():
        skip_col = tcol[TAPS][:8]

        def short(z, carry):
            before, jm = carry

            @pl.when(z == plane)
            def _():
                wait_for(recvb.at[pl.ds(0, 3)], in_recv.at[z])

            @pl.when(z != plane)
            def _():
                wait_for(recvb.at[pl.ds(0, 4)], in_recv.at[z])

            for b4 in range(4):
                b = 4 * z + b4
                x = recvb[b].astype(F32)
                total = tcol[0] * x
                turned = []
                for j in range(1, TAPS):
                    t = pltpu.roll(x, j, 1)
                    total = total + tcol[j] * jnp.where(lane < j, before[j - 1], t)
                    turned.append(t)
                conv_s[b] = total
                pb_s[b] = (total[:8] * total[8:]).astype(BF16).astype(F32)
                before = tuple(turned)

            pb4 = pb_s[pl.ds(4 * z, 4)]
            pj4 = dot(pb4.reshape(32, BLK).astype(BF16), flip).reshape(4, 8, BLK)
            for half in range(2):
                e = 2 * z + half
                p0, p1 = pb4[2 * half], pb4[2 * half + 1]
                j0, j1 = pj4[2 * half], pj4[2 * half + 1]
                r8_s[PAIRS - 1 - e] = jnp.where(low_rows, p0, half_turn(p1))
                gg_s[PAIRS - 1 - e, :, :BLK] = jnp.where(low_rows, half_turn(j0), j1)
                gg_s[PAIRS - 1 - e, :, BLK:] = jnp.where(low_rows, half_turn(jm), j0)
                z_s[e, 4:, :BLK] = p0[4:]
                z_s[e, 4:, BLK:] = p1[4:]
                z_s[PAIRS - 1 - e, :4, :BLK] = j1[:4]
                z_s[PAIRS - 1 - e, :4, BLK:] = j0[:4]
                jm = j1
            return before, jm

        empty = tuple(jnp.zeros((16, BLK), F32) for _ in range(TAPS - 1))
        lax.fori_loop(0, NB // 4, short, (empty, jnp.zeros((8, BLK), F32)))

        r8_t = dot(identity, r8_s[...].reshape(256, BLK).astype(BF16), ((1,), (1,))).astype(BF16)
        inside = square_lane <= square_row

        for odd in range(2):
            ggb[odd] = gg_s[odd : odd + 40].reshape(320, 2 * BLK).astype(BF16)

        def fold(x):
            return jnp.sum(x.reshape(BLK // 8, 8, BLK), axis=0)

        within = None
        for f in range(PAIRS):
            depth = 256 if f < 8 else 128
            first = 8 * (f - f % 2)
            product = dot(r8_t[:, :depth], ggb[f % 2, first : first + depth, :])
            for half in range(2):
                n = 2 * f + half
                turned = pltpu.roll(
                    product[:, half * BLK : (half + 1) * BLK], 1, 1, stride=1, stride_axis=0
                )
                everything = fold(turned)
                next_within = fold(jnp.where(inside, turned, 0.0))
                if n > 0:
                    fbuf[n - 1] = jnp.sum(
                        within + (everything - next_within), axis=0, keepdims=True
                    )
                within = next_within
        fbuf[NB - 1] = jnp.sum(within, axis=0, keepdims=True)

        for i in range(1, 4):
            other = lax.rem(part + i, 4)
            remote(
                fbuf.at[pl.ds(QUART * other, QUART)], frecv.at[part],
                fr_send, fr_recv, 4 * plane + other,
            ).start()
        frecv[part] = fbuf[pl.ds(QUART * part, QUART)]

        zb[...] = z_s[...].reshape(PAIRS * 8, 2 * BLK).astype(BF16)
        for d in range(PAIRS):
            t0, t1, t2 = toep[2 * d], toep[2 * d + 1], toep[2 * d + 2]
            weights = jnp.concatenate(
                [jnp.concatenate([t1, t2], axis=1), jnp.concatenate([t0, t1], axis=1)], axis=0
            )
            term = dot(zb[: 8 * (PAIRS - d), :], weights).reshape(PAIRS - d, 8, 2 * BLK)
            if d == 0:
                y_s[...] = term
            else:
                y_s[d:] += term

        wait_for(frecv.at[pl.ds(0, 3)], fr_recv)
        for n in range(QUART):
            fqf[n : n + 1, :] = lag_scale * (
                (frecv[0, n] + frecv[1, n]) + (frecv[2, n] + frecv[3, n])
            )
        fqf[QUART:, :] = jnp.zeros((16 - QUART, BLK), F32)
        fq[...] = fqf[...].astype(BF16)

        for half in range(2):
            y = y_s[:, :, half * BLK : (half + 1) * BLK].reshape(PAIRS * 8, BLK)
            high = y.astype(BF16)
            rest = (y - high.astype(F32)).astype(BF16)
            yj_s[:, :, half * BLK : (half + 1) * BLK] = (
                dot(high, flip) + dot(rest, flip)
            ).reshape(PAIRS, 8, BLK)

        for zp in range(NB // 4):
            @pl.when(zp != plane)
            def _(zp=zp):
                remote(fq, fgbuf.at[part, plane], fb_send, fb_recv, 4 * zp + part).start()

        fgbuf[part, plane] = fq[...]

        def gates(b, y, yj):
            p = pb_s[b]
            u = half_turn(jnp.where(low_rows, yj, y) + skip_col * p)
            short_tile = conv_s[b]
            he = jnp.concatenate([short_tile[8:] * u, short_tile[:8] * u], axis=0)
            turned = tuple(pltpu.roll(he, BLK - j, 1) for j in range(1, TAPS))
            return he, turned, p * half_turn(p)

        def finish(he, turned, x, following, sums):
            total = tcol[0] * he
            new_sums = [sums[0] + he * x]
            for j in range(1, TAPS):
                s = jnp.where(lane < BLK - j, turned[j - 1], following[j - 1])
                total = total + tcol[j] * s
                new_sums.append(sums[j] + s * x)
            return total.astype(BF16), tuple(new_sums)

        def send_plane(zp):
            for b4 in range(4):
                b = 4 * zp + b4

                @pl.when(b != me)
                def _(b=b):
                    remote(retb.at[b + 1], retr.at[me], ret_send, ret_recv, b).start()

        def post(zp, carry):
            he, turned, x, sums, skip_sum = carry
            for b4 in range(4):
                b = 4 * zp + b4
                y_half = slice(BLK, None) if b4 % 2 else slice(0, BLK)
                j_half = slice(0, BLK) if b4 % 2 else slice(BLK, None)
                e = 2 * zp + b4 // 2
                new_he, following, skip_term = gates(
                    b, y_s[e, :, y_half], yj_s[PAIRS - 1 - e, :, j_half]
                )
                retb[b], sums = finish(he, turned, x, following, sums)
                he, turned, x = new_he, following, recvb[b].astype(F32)
                skip_sum = skip_sum + skip_term

            @pl.when((zp > 0) & (zp < 7))
            def _():
                send_plane(zp - 1)

            return he, turned, x, sums, skip_sum

        zero = jnp.zeros((16, BLK), F32)
        start = (zero, empty, zero, (zero,) * TAPS, jnp.zeros((8, BLK), F32))
        he, turned, x, sums, skip_sum = lax.fori_loop(0, NB // 4, post, start)
        retb[NB], sums = finish(he, turned, x, empty, sums)

        line = jnp.zeros((16, BLK), F32)
        for j in range(TAPS):
            line = line + jnp.where(
                lane == 16 * j + row, jnp.sum(sums[j], axis=1, keepdims=True), 0.0
            )
        skip_line = jnp.where(
            lane[:8] == 16 * TAPS + row[:8], jnp.sum(skip_sum, axis=1, keepdims=True), 0.0
        )
        small[...] = tap_scale * (
            jnp.sum(line, axis=0, keepdims=True) + jnp.sum(skip_line, axis=0, keepdims=True)
        )
        send_plane(6)

        def spread_small(i, carry):
            @pl.when(i != me)
            def _():
                remote(small, smallr.at[me], sm_send, sm_recv, i).start()

            return carry

        lax.fori_loop(0, NB // 2, spread_small, 0)
        wait_for(fgbuf.at[0, pl.ds(0, NG - 1)], fb_recv)
        forward_lags()
        for zp in range(7, NB // 4):
            send_plane(zp)
        lax.fori_loop(NB // 2, NB, spread_small, 0)
        retr[me] = retb[me + 1]
        smallr[me] = small[...]

    @pl.when(me >= NW)
    def _():
        wait_for(fgbuf.at[0], fb_recv)
        forward_lags()

    outs = [
        pltpu.make_async_copy(retr, back_hbm, out_sem.at[0]),
        pltpu.make_async_copy(smallr, small_hbm, out_sem.at[1]),
        pltpu.make_async_copy(fgbuf, fg_hbm, out_sem.at[2]),
    ]
    for out, buffer, sem in zip(outs[:2], (retr, smallr), (ret_recv, sm_recv)):
        @pl.when(working)
        def _(buffer=buffer, sem=sem):
            wait_for(buffer.at[pl.ds(0, NW - 1)], sem)

        @pl.when(me >= NW)
        def _(buffer=buffer, sem=sem):
            wait_for(buffer, sem)

        out.start()
    wait_for(fgbuf.at[pl.ds(0, 3)], fx_recv)
    outs[2].start()

    @pl.when(working)
    def _drain():
        wait_for(sendb.at[pl.ds(0, NW - 1)], in_send)
        wait_for(frecv.at[pl.ds(0, 3)], fr_send)
        wait_for(retb.at[pl.ds(0, NB - 1)], ret_send)
        wait_for(fbuf.at[pl.ds(0, NB - 1)], sm_send)
        wait_for(fgbuf.at[0], fb_send)
        wait_for(fgbuf.at[0, pl.ds(0, 3)], fb_send)

    @pl.when(me >= NW)
    def _():
        wait_for(sendb, in_send)

    wait_for(fgbuf.at[pl.ds(0, 3)], fx_send)
    for out in outs:
        out.wait()


def assemble(
    back_hbm, small_hbm, fg_hbm,
    out_ref, ig_ref, tapg_ref, skipg_ref, fg_ref,
    backb, smallb, fgbuf, fg_s, sm_s, sems,
):
    loads = [
        pltpu.make_async_copy(back_hbm, backb, sems.at[0]),
        pltpu.make_async_copy(small_hbm, smallb, sems.at[1]),
        pltpu.make_async_copy(fg_hbm, fgbuf, sems.at[2]),
    ]
    for load in loads:
        load.start()
    perm = transposer()
    loads[0].wait()
    back = dot(backb[...].reshape(512, BLK), perm, ((0,), (0,))).astype(BF16)
    ig_ref[0] = back[:, 0:128]
    ig_ref[1] = back[:, 128:256]
    out_ref[...] = back[:, 256:384]
    ig_ref[2] = back[:, 384:512]

    loads[1].wait()
    sm_s[...] = jnp.zeros((BLK, BLK), F32)
    for m in range(NW):
        sm_s[m : m + 1, :] = smallb[m]
    select = jnp.where(iota((BLK, BLK), 0) == iota((BLK, BLK), 1) // 4, 1.0, 0.0)
    spread = lax.dot_general(
        sm_s[...].T, select, (((1,), (0,)), ((), ())),
        precision=lax.Precision.HIGHEST, preferred_element_type=F32,
    ).reshape(8, 16, BLK)
    row3 = iota((8, 16, BLK), 1)
    channel = iota((8, 16, BLK), 2) % 4
    for stream, first in enumerate((0, 4, 12)):
        picked = jnp.sum(jnp.where(row3 == channel + first, spread, 0.0), axis=1)
        tapg_ref[stream] = picked[:TAPS]
        if stream == 0:
            skipg_ref[...] = picked[TAPS:]

    loads[2].wait()
    fg_s[...] = fgbuf[...].astype(F32)
    for part in range(4):
        def lay(n, carry, part=part):
            at = pl.ds(pl.multiple_of((QUART * part + n) * BLK, BLK), BLK)
            for g in range(NG):
                fg_ref[g : g + 1, at] = fg_s[part, g, pl.ds(n, 1), :]
            return carry

        lax.fori_loop(0, QUART, lay, 0)


def local(query_in, key_in, value_in, short_taps, long_filters, skip_gain, cotangent):
    vmem = pl.BlockSpec(memory_space=pltpu.VMEM)
    anywhere = pl.BlockSpec(memory_space=pl.ANY)
    dma = pltpu.SemaphoreType.DMA
    raw = (
        jax.ShapeDtypeStruct((NW, 16, BLK), BF16),
        jax.ShapeDtypeStruct((NW, 1, BLK), F32),
        jax.ShapeDtypeStruct((4, NG, 16, BLK), BF16),
    )
    back, small, lag_rows = pl.pallas_call(
        kernel,
        out_shape=raw,
        in_specs=[pl.BlockSpec(memory_space=pltpu.HBM)] * 7,
        out_specs=(anywhere,) * 3,
        scratch_shapes=[
            pltpu.VMEM((4, BLK, BLK), BF16),
            pltpu.VMEM((3, TAPS, BLK), F32),
            pltpu.VMEM((NG, NB * BLK), BF16),
            pltpu.VMEM((1, BLK), F32),
            pltpu.VMEM((512, 512), BF16),
            pltpu.VMEM((NW, 16, BLK), BF16),
            pltpu.VMEM((NB, 16, BLK), BF16),
            pltpu.VMEM((NB + 1, BLK, BLK), BF16),
            pltpu.VMEM((TAPS + 1, 16, BLK), F32),
            pltpu.VMEM((NB, 16, BLK), F32),
            pltpu.VMEM((NB, 8, BLK), F32),
            pltpu.VMEM((32, 8, BLK), F32),
            pltpu.VMEM((42, 8, 2 * BLK), F32),
            pltpu.VMEM((2, 320, 2 * BLK), BF16),
            pltpu.VMEM((PAIRS, 8, 2 * BLK), F32),
            pltpu.VMEM((PAIRS * 8, 2 * BLK), BF16),
            pltpu.VMEM((PAIRS, 8, 2 * BLK), F32),
            pltpu.VMEM((PAIRS, 8, 2 * BLK), F32),
            pltpu.VMEM((NB + 1, 16, BLK), BF16),
            pltpu.VMEM((NW, 16, BLK), BF16),
            pltpu.VMEM((1, BLK), F32),
            pltpu.VMEM((NW, 1, BLK), F32),
            pltpu.VMEM((NB, 1, BLK), F32),
            pltpu.VMEM((4, QUART, 1, BLK), F32),
            pltpu.VMEM((16, BLK), F32),
            pltpu.VMEM((16, BLK), BF16),
            pltpu.VMEM((4, NG, 16, BLK), BF16),
            dma((7,)), dma((3,)), dma(()), dma((NB // 4,)), dma(()), dma(()), dma(()), dma(()),
            dma(()), dma(()), dma(()), dma(()), dma(()), dma(()),
            pltpu.SemaphoreType.REGULAR((NW // 4,)),
        ],
        compiler_params=pltpu.CompilerParams(
            collective_id=0, has_side_effects=True, vmem_limit_bytes=24 << 20
        ),
        name="hyena",
    )(*(
        pltpu.with_memory_space_constraint(x, pltpu.HBM)
        for x in (
            query_in, key_in, cotangent, value_in, short_taps, long_filters,
            skip_gain.reshape(1, BLK),
        )
    ))
    block_out, input_grads, tap_grads, skip_grad, filter_grad = pl.pallas_call(
        assemble,
        out_shape=(
            jax.ShapeDtypeStruct((BLK, BLK), BF16),
            jax.ShapeDtypeStruct((3, BLK, BLK), BF16),
            jax.ShapeDtypeStruct((3, TAPS, BLK), F32),
            jax.ShapeDtypeStruct((1, BLK), F32),
            jax.ShapeDtypeStruct((NG, NB * BLK), F32),
        ),
        in_specs=[anywhere] * 3,
        out_specs=(vmem,) * 5,
        scratch_shapes=[
            pltpu.VMEM((NW, 16, BLK), BF16),
            pltpu.VMEM((NW, 1, BLK), F32),
            pltpu.VMEM((4, NG, 16, BLK), BF16),
            pltpu.VMEM((4, NG, 16, BLK), F32),
            pltpu.VMEM((BLK, BLK), F32),
            dma((3,)),
        ],
        compiler_params=pltpu.CompilerParams(vmem_limit_bytes=8 << 20),
        name="assemble",
    )(back, small, lag_rows)
    return block_out, input_grads, tap_grads, skip_grad.reshape(BLK), filter_grad


def solution(mesh):
    in_specs = (
        P("seq", "chan"),
        P("seq", "chan"),
        P("seq", "chan"),
        P(None, None, "chan"),
        P("chan", None),
        P("chan"),
        P("seq", "chan"),
    )
    out_specs = (
        P("seq", "chan"),
        P(None, "seq", "chan"),
        P(None, None, "chan"),
        P("chan"),
        P("chan", None),
    )
    return jax.shard_map(local, mesh=mesh, in_specs=in_specs, out_specs=out_specs, check_vma=False)
```

```python
import math

import jax
import jax.numpy as jnp
from jax import lax
from jax.experimental import pallas as pl
from jax.experimental.pallas import tpu as pltpu
from jax.sharding import PartitionSpec as P

F32 = jnp.float32
BF16 = jnp.bfloat16
MESH = pl.DeviceIdType.MESH

BLK = 128
NB = 48
NW = 32
TAPS = 7
NG = 8
QUART = NB // 4
PAIRS = NB // 2


def iota(shape, dim):
    return lax.broadcasted_iota(jnp.int32, shape, dim)


def dot(a, b, dims=((1,), (0,))):
    return lax.dot_general(a, b, (dims, ((), ())), preferred_element_type=F32)


def half_turn(x):
    return pltpu.roll(x, 4, 0)


def remote(src, dst, send_sem, recv_sem, target):
    return pltpu.make_async_remote_copy(
        src_ref=src,
        dst_ref=dst,
        send_sem=send_sem,
        recv_sem=recv_sem,
        device_id={"seq": target},
        device_id_type=MESH,
    )


def wait_for(ref, sem):
    pltpu.make_async_copy(ref, ref, sem).wait()


def transposer():
    rho = iota((512, 1), 0)
    column = 128 * ((rho // 4) % 4) + 4 * (rho // 16) + rho % 4
    return jnp.where(iota((512, 512), 1) == column, 1.0, 0.0).astype(BF16)


def kernel(
    q_hbm, k_hbm, c_hbm, v_hbm, taps_hbm, filt_hbm, skip_hbm,
    back_hbm, small_hbm, fg_hbm,
    streams, taps_ref, filt_ref, skip_ref,
    perm, sendb, recvb, toep, tcol, conv_s, pb_s, r8_s, gg_s, ggb, z_s, zb, y_s, yj_s,
    retb, retr, small, smallr, fbuf, frecv, fqf, fq, fgbuf,
    load_sem, out_sem, in_send, in_recv, ret_send, ret_recv, sm_send, sm_recv,
    fr_send, fr_recv, fb_send, fb_recv, fx_send, fx_recv, ready,
):
    me = lax.axis_index("seq")
    plane = me // 4
    part = me % 4
    tap_scale = 1.0 / math.sqrt(NB * BLK)
    lag_scale = 1.0 / math.sqrt(NB * BLK * 16)
    working = me < NW
    barrier = pltpu.get_barrier_semaphore()

    loads = [
        pltpu.make_async_copy(source, streams.at[r], load_sem.at[r])
        for r, source in enumerate((q_hbm, k_hbm, c_hbm, v_hbm))
    ]
    for load in loads:
        load.start()
    own_loads = [
        pltpu.make_async_copy(taps_hbm, taps_ref, load_sem.at[4]),
        pltpu.make_async_copy(filt_hbm, filt_ref, load_sem.at[5]),
        pltpu.make_async_copy(skip_hbm, skip_ref, load_sem.at[6]),
    ]

    @pl.when(working)
    def _greet():
        for load in own_loads:
            load.start()

        def greet(i, carry):
            @pl.when(i != me)
            def _():
                pl.semaphore_signal(barrier, inc=1, device_id={"seq": i}, device_id_type=MESH)

            return carry

        lax.fori_loop(4 * plane, NB, greet, 0)

    perm[...] = transposer()
    for load in loads:
        load.wait()
    joined = jnp.concatenate([streams[r] for r in range(4)], axis=1)
    sendb[...] = dot(perm[...], joined, ((1,), (1,))).astype(BF16).reshape(NW, 16, BLK)

    lane = iota((16, BLK), 1)
    row = iota((16, BLK), 0)
    low_rows = iota((8, BLK), 0) < 4
    square_row = iota((BLK, BLK), 0)
    square_lane = iota((BLK, BLK), 1)
    identity = jnp.where(square_row == square_lane, 1.0, 0.0).astype(BF16)
    flip = jnp.where(square_row + square_lane == BLK - 1, 1.0, 0.0).astype(BF16)

    def send_in(zp):
        for m in range(4 * zp, 4 * zp + 4):
            @pl.when(m != me)
            def _(m=m):
                remote(sendb.at[m], recvb.at[me], in_send, in_recv.at[plane], m).start()

    @pl.when(working)
    def _():
        pl.semaphore_wait(barrier, 4 * plane + 3)

        def tell(i, carry):
            pl.semaphore_signal(
                ready.at[plane], inc=1, device_id={"seq": i}, device_id_type=MESH
            )
            return carry

        lax.fori_loop(0, 4 * plane, tell, 0)

    @pl.when(me >= NW)
    def _():
        pl.semaphore_wait(barrier, NW)

    for zp in reversed(range(NW // 4)):
        @pl.when(zp <= plane)
        def _(zp=zp):
            send_in(zp)

    @pl.when(working)
    def _prepare():
        for load in own_loads:
            load.wait()

        own = lane == 4 * me + row % 4
        for j in range(TAPS):
            q_tap = jnp.broadcast_to(taps_ref[0, j : j + 1, :], (16, BLK))
            k_tap = jnp.broadcast_to(taps_ref[1, j : j + 1, :], (16, BLK))
            v_tap = jnp.broadcast_to(taps_ref[2, j : j + 1, :], (16, BLK))
            tap = jnp.where(row < 4, q_tap, jnp.where(row < 8, k_tap, v_tap))
            column = jnp.sum(jnp.where(own, tap, 0.0), axis=1, keepdims=True)
            column = jnp.broadcast_to(column, (16, BLK))
            unit = 1.0 if j == 0 else 0.0
            tcol[j] = jnp.where((row >= 8) & (row < 12), unit, column)
        skip_own = jnp.where(own, jnp.broadcast_to(skip_ref[...], (16, BLK)), 0.0)
        tcol[TAPS] = jnp.broadcast_to(jnp.sum(skip_own, axis=1, keepdims=True), (16, BLK))

        toep[0] = jnp.zeros((BLK, BLK), BF16)

        def build(n, previous):
            rows = filt_ref[:, pl.ds(pl.multiple_of(n * BLK, BLK), BLK)].astype(F32)
            line = jnp.sum(jnp.where(iota((NG, BLK), 0) == plane, rows, 0.0), axis=0, keepdims=True)
            turned = pltpu.roll(
                jnp.broadcast_to(line, (BLK, BLK)), 0, 1, stride=1, stride_axis=0
            )
            toep[n + 1] = jnp.where(square_lane >= square_row, turned, previous).astype(BF16)
            return turned

        lax.fori_loop(0, NB, build, jnp.zeros((BLK, BLK), F32), unroll=2)

        r8_s[PAIRS:] = jnp.zeros((32 - PAIRS, 8, BLK), F32)
        gg_s[PAIRS:] = jnp.zeros((42 - PAIRS, 8, 2 * BLK), F32)
        recvb[me] = sendb[me]

    for zp in range(1, NW // 4):
        @pl.when(zp > plane)
        def _(zp=zp):
            pl.semaphore_wait(ready.at[zp], 4)
            send_in(zp)

    def forward_lags():
        for i in range(1, 4):
            other = lax.rem(part + i, 4)
            remote(fgbuf.at[part], fgbuf.at[part], fx_send, fx_recv, 4 * plane + other).start()

    @pl.when(working)
    def _work():
        skip_col = tcol[TAPS][:8]

        def short(z, carry):
            before, jm = carry

            @pl.when(z == plane)
            def _():
                wait_for(recvb.at[pl.ds(0, 3)], in_recv.at[z])

            @pl.when(z != plane)
            def _():
                wait_for(recvb.at[pl.ds(0, 4)], in_recv.at[z])

            for b4 in range(4):
                b = 4 * z + b4
                x = recvb[b].astype(F32)
                total = tcol[0] * x
                turned = []
                for j in range(1, TAPS):
                    t = pltpu.roll(x, j, 1)
                    total = total + tcol[j] * jnp.where(lane < j, before[j - 1], t)
                    turned.append(t)
                conv_s[b] = total
                pb_s[b] = (total[:8] * total[8:]).astype(BF16).astype(F32)
                before = tuple(turned)

            pb4 = pb_s[pl.ds(4 * z, 4)]
            pj4 = dot(pb4.reshape(32, BLK).astype(BF16), flip).reshape(4, 8, BLK)
            for half in range(2):
                e = 2 * z + half
                p0, p1 = pb4[2 * half], pb4[2 * half + 1]
                j0, j1 = pj4[2 * half], pj4[2 * half + 1]
                r8_s[PAIRS - 1 - e] = jnp.where(low_rows, p0, half_turn(p1))
                gg_s[PAIRS - 1 - e, :, :BLK] = jnp.where(low_rows, half_turn(j0), j1)
                gg_s[PAIRS - 1 - e, :, BLK:] = jnp.where(low_rows, half_turn(jm), j0)
                z_s[e, 4:, :BLK] = p0[4:]
                z_s[e, 4:, BLK:] = p1[4:]
                z_s[PAIRS - 1 - e, :4, :BLK] = j1[:4]
                z_s[PAIRS - 1 - e, :4, BLK:] = j0[:4]
                jm = j1
            return before, jm

        empty = tuple(jnp.zeros((16, BLK), F32) for _ in range(TAPS - 1))
        lax.fori_loop(0, NB // 4, short, (empty, jnp.zeros((8, BLK), F32)))

        r8_t = dot(identity, r8_s[...].reshape(256, BLK).astype(BF16), ((1,), (1,))).astype(BF16)
        inside = square_lane <= square_row

        for odd in range(2):
            ggb[odd] = gg_s[odd : odd + 40].reshape(320, 2 * BLK).astype(BF16)

        def fold(x):
            return jnp.sum(x.reshape(BLK // 8, 8, BLK), axis=0)

        within = None
        for f in range(PAIRS):
            depth = 256 if f < 8 else 128
            first = 8 * (f - f % 2)
            product = dot(r8_t[:, :depth], ggb[f % 2, first : first + depth, :])
            for half in range(2):
                n = 2 * f + half
                turned = pltpu.roll(
                    product[:, half * BLK : (half + 1) * BLK], 1, 1, stride=1, stride_axis=0
                )
                everything = fold(turned)
                next_within = fold(jnp.where(inside, turned, 0.0))
                if n > 0:
                    fbuf[n - 1] = jnp.sum(
                        within + (everything - next_within), axis=0, keepdims=True
                    )
                within = next_within
        fbuf[NB - 1] = jnp.sum(within, axis=0, keepdims=True)

        for i in range(1, 4):
            other = lax.rem(part + i, 4)
            remote(
                fbuf.at[pl.ds(QUART * other, QUART)], frecv.at[part],
                fr_send, fr_recv, 4 * plane + other,
            ).start()
        frecv[part] = fbuf[pl.ds(QUART * part, QUART)]

        zb[...] = z_s[...].reshape(PAIRS * 8, 2 * BLK).astype(BF16)
        for d in range(PAIRS):
            t0, t1, t2 = toep[2 * d], toep[2 * d + 1], toep[2 * d + 2]
            weights = jnp.concatenate(
                [jnp.concatenate([t1, t2], axis=1), jnp.concatenate([t0, t1], axis=1)], axis=0
            )
            term = dot(zb[: 8 * (PAIRS - d), :], weights).reshape(PAIRS - d, 8, 2 * BLK)
            if d == 0:
                y_s[...] = term
            else:
                y_s[d:] += term

        wait_for(frecv.at[pl.ds(0, 3)], fr_recv)
        for n in range(QUART):
            fqf[n : n + 1, :] = lag_scale * (
                (frecv[0, n] + frecv[1, n]) + (frecv[2, n] + frecv[3, n])
            )
        fqf[QUART:, :] = jnp.zeros((16 - QUART, BLK), F32)
        fq[...] = fqf[...].astype(BF16)

        for half in range(2):
            y = y_s[:, :, half * BLK : (half + 1) * BLK].reshape(PAIRS * 8, BLK)
            high = y.astype(BF16)
            rest = (y - high.astype(F32)).astype(BF16)
            yj_s[:, :, half * BLK : (half + 1) * BLK] = (
                dot(high, flip) + dot(rest, flip)
            ).reshape(PAIRS, 8, BLK)

        for zp in range(NB // 4):
            @pl.when(zp != plane)
            def _(zp=zp):
                remote(fq, fgbuf.at[part, plane], fb_send, fb_recv, 4 * zp + part).start()

        fgbuf[part, plane] = fq[...]

        def gates(b, y, yj):
            p = pb_s[b]
            u = half_turn(jnp.where(low_rows, yj, y) + skip_col * p)
            short_tile = conv_s[b]
            he = jnp.concatenate([short_tile[8:] * u, short_tile[:8] * u], axis=0)
            turned = tuple(pltpu.roll(he, BLK - j, 1) for j in range(1, TAPS))
            return he, turned, p * half_turn(p)

        def finish(he, turned, x, following, sums):
            total = tcol[0] * he
            new_sums = [sums[0] + he * x]
            for j in range(1, TAPS):
                s = jnp.where(lane < BLK - j, turned[j - 1], following[j - 1])
                total = total + tcol[j] * s
                new_sums.append(sums[j] + s * x)
            return total.astype(BF16), tuple(new_sums)

        def send_plane(zp):
            for b4 in range(4):
                b = 4 * zp + b4

                @pl.when(b != me)
                def _(b=b):
                    remote(retb.at[b + 1], retr.at[me], ret_send, ret_recv, b).start()

        def post(zp, carry):
            he, turned, x, sums, skip_sum = carry
            for b4 in range(4):
                b = 4 * zp + b4
                y_half = slice(BLK, None) if b4 % 2 else slice(0, BLK)
                j_half = slice(0, BLK) if b4 % 2 else slice(BLK, None)
                e = 2 * zp + b4 // 2
                new_he, following, skip_term = gates(
                    b, y_s[e, :, y_half], yj_s[PAIRS - 1 - e, :, j_half]
                )
                retb[b], sums = finish(he, turned, x, following, sums)
                he, turned, x = new_he, following, recvb[b].astype(F32)
                skip_sum = skip_sum + skip_term

            @pl.when((zp > 0) & (zp < 7))
            def _():
                send_plane(zp - 1)

            return he, turned, x, sums, skip_sum

        zero = jnp.zeros((16, BLK), F32)
        start = (zero, empty, zero, (zero,) * TAPS, jnp.zeros((8, BLK), F32))
        he, turned, x, sums, skip_sum = lax.fori_loop(0, NB // 4, post, start)
        retb[NB], sums = finish(he, turned, x, empty, sums)

        line = jnp.zeros((16, BLK), F32)
        for j in range(TAPS):
            line = line + jnp.where(
                lane == 16 * j + row, jnp.sum(sums[j], axis=1, keepdims=True), 0.0
            )
        skip_line = jnp.where(
            lane[:8] == 16 * TAPS + row[:8], jnp.sum(skip_sum, axis=1, keepdims=True), 0.0
        )
        small[...] = tap_scale * (
            jnp.sum(line, axis=0, keepdims=True) + jnp.sum(skip_line, axis=0, keepdims=True)
        )
        send_plane(6)

        def spread_small(i, carry):
            @pl.when(i != me)
            def _():
                remote(small, smallr.at[me], sm_send, sm_recv, i).start()

            return carry

        lax.fori_loop(0, NB // 2, spread_small, 0)
        wait_for(fgbuf.at[0, pl.ds(0, NG - 1)], fb_recv)
        forward_lags()
        for zp in range(7, NB // 4):
            send_plane(zp)
        lax.fori_loop(NB // 2, NB, spread_small, 0)
        retr[me] = retb[me + 1]
        smallr[me] = small[...]

    @pl.when(me >= NW)
    def _():
        wait_for(fgbuf.at[0], fb_recv)
        forward_lags()

    outs = [
        pltpu.make_async_copy(retr, back_hbm, out_sem.at[0]),
        pltpu.make_async_copy(smallr, small_hbm, out_sem.at[1]),
        pltpu.make_async_copy(fgbuf, fg_hbm, out_sem.at[2]),
    ]
    for out, buffer, sem in zip(outs[:2], (retr, smallr), (ret_recv, sm_recv)):
        @pl.when(working)
        def _(buffer=buffer, sem=sem):
            wait_for(buffer.at[pl.ds(0, NW - 1)], sem)

        @pl.when(me >= NW)
        def _(buffer=buffer, sem=sem):
            wait_for(buffer, sem)

        out.start()
    wait_for(fgbuf.at[pl.ds(0, 3)], fx_recv)
    outs[2].start()

    @pl.when(working)
    def _drain():
        wait_for(sendb.at[pl.ds(0, NW - 1)], in_send)
        wait_for(frecv.at[pl.ds(0, 3)], fr_send)
        wait_for(retb.at[pl.ds(0, NB - 1)], ret_send)
        wait_for(fbuf.at[pl.ds(0, NB - 1)], sm_send)
        wait_for(fgbuf.at[0], fb_send)
        wait_for(fgbuf.at[0, pl.ds(0, 3)], fb_send)

    @pl.when(me >= NW)
    def _():
        wait_for(sendb, in_send)

    wait_for(fgbuf.at[pl.ds(0, 3)], fx_send)
    for out in outs:
        out.wait()


def assemble(
    backb, smallb, fgbuf,
    out_ref, ig_ref, tapg_ref, skipg_ref, fg_ref,
    fg_s, sm_s,
):
    perm = transposer()
    back = dot(backb[...].reshape(512, BLK), perm, ((0,), (0,))).astype(BF16)
    ig_ref[0] = back[:, 0:128]
    ig_ref[1] = back[:, 128:256]
    out_ref[...] = back[:, 256:384]
    ig_ref[2] = back[:, 384:512]

    sm_s[...] = jnp.zeros((BLK, BLK), F32)
    for m in range(NW):
        sm_s[m : m + 1, :] = smallb[m]
    select = jnp.where(iota((BLK, BLK), 0) == iota((BLK, BLK), 1) // 4, 1.0, 0.0)
    spread = lax.dot_general(
        sm_s[...].T, select, (((1,), (0,)), ((), ())),
        precision=lax.Precision.HIGHEST, preferred_element_type=F32,
    ).reshape(8, 16, BLK)
    row3 = iota((8, 16, BLK), 1)
    channel = iota((8, 16, BLK), 2) % 4
    for stream, first in enumerate((0, 4, 12)):
        picked = jnp.sum(jnp.where(row3 == channel + first, spread, 0.0), axis=1)
        tapg_ref[stream] = picked[:TAPS]
        if stream == 0:
            skipg_ref[...] = picked[TAPS:]

    fg_s[...] = fgbuf[...].astype(F32)
    for part in range(4):
        def lay(n, carry, part=part):
            at = pl.ds(pl.multiple_of((QUART * part + n) * BLK, BLK), BLK)
            for g in range(NG):
                fg_ref[g : g + 1, at] = fg_s[part, g, pl.ds(n, 1), :]
            return carry

        lax.fori_loop(0, QUART, lay, 0)


def local(query_in, key_in, value_in, short_taps, long_filters, skip_gain, cotangent):
    vmem = pl.BlockSpec(memory_space=pltpu.VMEM)
    anywhere = pl.BlockSpec(memory_space=pl.ANY)
    dma = pltpu.SemaphoreType.DMA
    raw = (
        jax.ShapeDtypeStruct((NW, 16, BLK), BF16),
        jax.ShapeDtypeStruct((NW, 1, BLK), F32),
        jax.ShapeDtypeStruct((4, NG, 16, BLK), BF16),
    )
    back, small, lag_rows = pl.pallas_call(
        kernel,
        out_shape=raw,
        in_specs=[pl.BlockSpec(memory_space=pltpu.HBM)] * 7,
        out_specs=(anywhere,) * 3,
        scratch_shapes=[
            pltpu.VMEM((4, BLK, BLK), BF16),
            pltpu.VMEM((3, TAPS, BLK), F32),
            pltpu.VMEM((NG, NB * BLK), BF16),
            pltpu.VMEM((1, BLK), F32),
            pltpu.VMEM((512, 512), BF16),
            pltpu.VMEM((NW, 16, BLK), BF16),
            pltpu.VMEM((NB, 16, BLK), BF16),
            pltpu.VMEM((NB + 1, BLK, BLK), BF16),
            pltpu.VMEM((TAPS + 1, 16, BLK), F32),
            pltpu.VMEM((NB, 16, BLK), F32),
            pltpu.VMEM((NB, 8, BLK), F32),
            pltpu.VMEM((32, 8, BLK), F32),
            pltpu.VMEM((42, 8, 2 * BLK), F32),
            pltpu.VMEM((2, 320, 2 * BLK), BF16),
            pltpu.VMEM((PAIRS, 8, 2 * BLK), F32),
            pltpu.VMEM((PAIRS * 8, 2 * BLK), BF16),
            pltpu.VMEM((PAIRS, 8, 2 * BLK), F32),
            pltpu.VMEM((PAIRS, 8, 2 * BLK), F32),
            pltpu.VMEM((NB + 1, 16, BLK), BF16),
            pltpu.VMEM((NW, 16, BLK), BF16),
            pltpu.VMEM((1, BLK), F32),
            pltpu.VMEM((NW, 1, BLK), F32),
            pltpu.VMEM((NB, 1, BLK), F32),
            pltpu.VMEM((4, QUART, 1, BLK), F32),
            pltpu.VMEM((16, BLK), F32),
            pltpu.VMEM((16, BLK), BF16),
            pltpu.VMEM((4, NG, 16, BLK), BF16),
            dma((7,)), dma((3,)), dma(()), dma((NB // 4,)), dma(()), dma(()), dma(()), dma(()),
            dma(()), dma(()), dma(()), dma(()), dma(()), dma(()),
            pltpu.SemaphoreType.REGULAR((NW // 4,)),
        ],
        compiler_params=pltpu.CompilerParams(
            collective_id=0, has_side_effects=True, vmem_limit_bytes=24 << 20
        ),
        name="hyena",
    )(*(
        pltpu.with_memory_space_constraint(x, pltpu.HBM)
        for x in (
            query_in, key_in, cotangent, value_in, short_taps, long_filters,
            skip_gain.reshape(1, BLK),
        )
    ))
    block_out, input_grads, tap_grads, skip_grad, filter_grad = pl.pallas_call(
        assemble,
        out_shape=(
            jax.ShapeDtypeStruct((BLK, BLK), BF16),
            jax.ShapeDtypeStruct((3, BLK, BLK), BF16),
            jax.ShapeDtypeStruct((3, TAPS, BLK), F32),
            jax.ShapeDtypeStruct((1, BLK), F32),
            jax.ShapeDtypeStruct((NG, NB * BLK), F32),
        ),
        in_specs=[vmem] * 3,
        out_specs=(vmem,) * 5,
        scratch_shapes=[
            pltpu.VMEM((4, NG, 16, BLK), F32),
            pltpu.VMEM((BLK, BLK), F32),
        ],
        compiler_params=pltpu.CompilerParams(vmem_limit_bytes=8 << 20),
        name="assemble",
    )(back, small, lag_rows)
    return block_out, input_grads, tap_grads, skip_grad.reshape(BLK), filter_grad


def solution(mesh):
    in_specs = (
        P("seq", "chan"),
        P("seq", "chan"),
        P("seq", "chan"),
        P(None, None, "chan"),
        P("chan", None),
        P("chan"),
        P("seq", "chan"),
    )
    out_specs = (
        P("seq", "chan"),
        P(None, "seq", "chan"),
        P(None, None, "chan"),
        P("chan"),
        P("chan", None),
    )
    return jax.shard_map(local, mesh=mesh, in_specs=in_specs, out_specs=out_specs, check_vma=False)
```
